512 devices in a mesh: wave: 64 (over x, z, core), field: 8 (over y).
Axes of the slice: x: 4, y: 8, z: 8, core: 2. Of those that a mesh axis runs over, the one named last changes fastest.
Arguments:
- spectral: float32 [640, 1281, 2, 80], P('wave', None, None, 'field'), may hold values from -0.0078125 to 0.0078125
- legendre: bfloat16 [640, 1281, 128], P('wave'), may hold values from -6 to 6
- wave_pairs: int32 [640], P('wave'), may hold values from 0 to 639, each once
- npoints: int32 [256], replicated, may hold values from 20 to 5136, as said below
- lat_rows: int32 [256], P('wave'), may hold values from 0 to 255, as said below
Outputs:
- grid: bfloat16 [2, 80, 659968], P(None, None, ('wave', 'field'))
The draws below stay inside these ranges and needn't reach their ends.
Inputs may be any that keep to these rules, and one draw needn't show every extreme that they name: Slot p holds wavenumbers wave_pairs[p] and 1279 - wave_pairs[p]; every wavenumber is held by exactly one slot. `npoints`: a latitude i rows from the nearer pole among 1280 has 4 i + 16 points; window latitudes 2 u and 2 u + 1 have 5156 points together. `lat_rows`: every window latitude appears once; the latitudes in slots 2 q and 2 q + 1 have 5156 points together.
All inputs are finite; a program needn't handle non-finite values.
Results may differ from the reference program's by a relative error of at most 0.0063.
Values may be sent and summed in bfloat16 or wider, within the bound.
No kernel may reach another device: no remote copies, remote signals or barrier semaphores. Data moves between devices by JAX's collectives and lax.ppermute only.
A program may use at most 192 MiB of HBM per device.

```python
import math
import jax
import jax.numpy as jnp
from jax import lax

TRUNC = 1279
HEMI = 1280
FIELDS = 80
LATS = 256
NH = 128
ROW_PAIR = 5156


def window_layout(key):
    quarter = LATS // 4
    others = jax.random.permutation(jax.random.fold_in(key, 11), HEMI // 2 - 1)[:quarter - 1] + 2
    short_rows = jnp.concatenate([jnp.ones((1,), jnp.int32), others.astype(jnp.int32)])
    northern = jnp.stack([short_rows, HEMI + 1 - short_rows], axis=1).reshape(-1)
    points = jnp.concatenate([4 * northern + 16, 4 * northern + 16])
    order = jax.random.permutation(jax.random.fold_in(key, 12), LATS // 2).astype(jnp.int32)
    flipped = jax.random.randint(jax.random.fold_in(key, 13), (LATS // 2,), 0, 2).astype(jnp.int32)
    latitudes = jnp.stack([2 * order + flipped, 2 * order + 1 - flipped], axis=1).reshape(-1)
    return (points.astype(jnp.int32), latitudes.astype(jnp.int32))


def draw_npoints(key, part):
    return window_layout(key)[0]


def draw_lat_rows(key, part):
    return window_layout(key)[1]


def shard_levels(key, shape, split, low, largest):
    def one(axis_at, blocks):
        steps = jax.random.uniform(jax.random.fold_in(jax.random.fold_in(key, 6), axis_at), (blocks,), jnp.float32, low / len(split), largest / len(split))
        return jnp.repeat(jnp.exp(steps), shape[axis_at] // blocks).reshape((-1,) + (1,) * (len(shape) - axis_at - 1))

    gain = one(*split[0])
    for cut in split[1:]:
        gain = gain * one(*cut)
    return gain


def scatter_about(rng, dims, deviation, bound, shards=(), held_as=jnp.bfloat16):
    result = jax.random.normal(rng, dims, jnp.float32) * deviation
    if len(shards) > 0:
        result = shard_levels(rng, dims, shards, -0.22, 0.18) * result
    return jnp.clip(result, min=-bound, max=bound).astype(held_as)


def setup_inputs(seed: int = 0) -> dict:
    keys = jax.random.split(jax.random.key(seed), 6)
    spectral = scatter_about(keys[0], ((TRUNC + 1) // 2, TRUNC + 2, 2, FIELDS), 0.0005, 0.0078125, ((0, 64), (3, 8)), jnp.float32)
    legendre = scatter_about(keys[1], ((TRUNC + 1) // 2, TRUNC + 2, NH), 1.0, 6.0, ((0, 64),))
    wave_pairs = jax.random.permutation(keys[2], (TRUNC + 1) // 2).astype(jnp.int32)
    npoints = draw_npoints(jax.random.fold_in(keys[5], 71), 0)
    lat_rows = draw_lat_rows(jax.random.fold_in(keys[5], 71), 0)
    return {"spectral": spectral, "legendre": legendre, "wave_pairs": wave_pairs, "npoints": npoints, "lat_rows": lat_rows}


def fourier_table(wave_rows, first_points, second_points, columns):
    first_lat = columns < first_points
    longitude = jnp.where(first_lat, columns, columns - first_points)
    lon_count = jnp.where(first_lat, first_points, second_points)
    phase_int = (wave_rows[:, None] * longitude[None, :]) % lon_count[None, :]
    angles = phase_int.astype(jnp.float32) * (2.0 * math.pi) / lon_count[None, :].astype(jnp.float32)
    real_rows = (jnp.arange(wave_rows.shape[0], dtype=jnp.int32) % 2 == 0)[:, None]
    signed = jnp.where(real_rows, jnp.cos(angles), -jnp.sin(angles))
    weight = jnp.where(wave_rows == 0, 1.0, 2.0).astype(jnp.float32)[:, None]
    resolved = 2 * wave_rows[:, None] < lon_count[None, :]
    cosines = jnp.where(resolved, weight * signed, 0.0).astype(jnp.bfloat16)
    return cosines, first_lat


def wave_layout(wave_pairs, truncation):
    high_wave = truncation - wave_pairs
    wave_rows = jnp.stack([wave_pairs, wave_pairs, high_wave, high_wave], axis=1).reshape(-1)
    deriv_scale = jnp.stack([wave_pairs, high_wave], axis=1).reshape(-1).astype(jnp.float32) / truncation
    return wave_rows, deriv_scale


def turn(coeffs, deriv_scale):
    pairs = coeffs.astype(jnp.float32).reshape(coeffs.shape[:-1] + (-1, 2))
    turned = jnp.stack([-pairs[..., 1], pairs[..., 0]], axis=-1) * deriv_scale[:, None]
    return turned.reshape(coeffs.shape).astype(jnp.bfloat16)


def synthesize(values, turned, cosines, first_lat):
    field_span = values.shape[1]
    stacked_lhs = jnp.concatenate([values, turned], axis=0).reshape(4 * field_span, values.shape[2])
    products = jnp.dot(stacked_lhs, cosines, preferred_element_type=jnp.float32)
    products = products.reshape(2, 2, field_span, cosines.shape[1])
    return jnp.where(first_lat[None, None, :], products[:, 0], products[:, 1]).astype(jnp.bfloat16)


def reference(spectral, legendre, wave_pairs, npoints, lat_rows):
    truncation = TRUNC
    coeffs = spectral.astype(jnp.bfloat16)
    row_index = jnp.arange(truncation + 2, dtype=jnp.int32)
    split_row = (truncation + 1 - wave_pairs)[:, None]
    low_rows = row_index[None, :] < split_row
    offset = jnp.where(low_rows, row_index[None, :], row_index[None, :] - split_row)
    parity_sign = jnp.where(offset % 2 == 0, 1.0, -1.0).astype(jnp.float32)
    low_weight = low_rows.astype(jnp.float32)

    def one_slot(items):
        table_rows, values, low_part, signs = items
        row_masks = jnp.stack([low_part, low_part * signs, 1.0 - low_part, (1.0 - low_part) * signs], axis=1)
        stacked = values.astype(jnp.float32)[:, None, :, :] * row_masks[:, :, None, None]
        return jnp.einsum('rhcf,rj->hjfc', stacked, table_rows.astype(jnp.float32), precision=lax.Precision.HIGHEST)

    parts = lax.map(one_slot, (legendre, coeffs, low_weight, parity_sign))
    slot_count = parts.shape[0]
    parts = parts.reshape(slot_count, 2, 2, NH, FIELDS, 2)
    fourier = jnp.transpose(parts, (2, 3, 4, 0, 1, 5)).reshape(2 * NH, FIELDS, 4 * slot_count)
    fourier_b = fourier.astype(jnp.bfloat16)
    wave_rows, deriv_scale = wave_layout(wave_pairs, truncation)
    turned = turn(fourier_b, deriv_scale)
    columns = jnp.arange(ROW_PAIR, dtype=jnp.int32)

    def one_row(pair_lats):
        points = jnp.take(npoints, pair_lats)
        cosines, first_lat = fourier_table(wave_rows, points[0], points[1], columns)
        return synthesize(jnp.take(fourier_b, pair_lats, axis=0), jnp.take(turned, pair_lats, axis=0), cosines, first_lat)

    rows_out = lax.map(one_row, lat_rows.reshape(-1, 2))
    return jnp.transpose(rows_out, (1, 2, 0, 3)).reshape(2, FIELDS, -1)
```

```python
import functools

import jax
import jax.numpy as jnp
import numpy as np
from jax import lax
from jax.experimental import pallas as pl
from jax.experimental.pallas import tpu as pltpu
from jax.sharding import PartitionSpec as P

ROW_PAIR = 5156
QUARTER = ROW_PAIR // 4
CHUNK = 256
PAIR_CHUNKS = 7
GROUPS = 5
TILES = 4
ROWS = 24
SIN = (6.283184905907144, -41.34158660945749, 81.59984497508991, -76.61321302879018, 41.33641025544816, -12.459753683550199)
COS = (0.999999988711474, -19.739204378854772, 64.93911099976975, -85.4500154366872, 60.16656814312298, -25.963448256110482, 6.5226306139218035)
f32, bf16, i32 = jnp.float32, jnp.bfloat16, jnp.int32


def legendre_kernel(truncation, waves, spec_ref, leg_ref, out_ref, coeffs):
    slot = pl.program_id(0)
    rows = truncation + 2
    fields = spec_ref.shape[1]

    @pl.when(slot == 0)
    def _():
        coeffs[...] = jnp.zeros_like(coeffs)

    for field in range(fields):
        coeffs[2 * field : 2 * field + 2, 0:rows] = spec_ref[0, field]
    split = truncation + 1 - waves[slot]
    row = lax.broadcasted_iota(i32, (1, rows), 1)
    low = row < split
    offset = jnp.where(low, row, row - split)
    sign = jnp.where(offset % 2 == 0, 1.0, -1.0).astype(f32)
    low = jnp.where(low, 1.0, 0.0).astype(f32)
    high = 1.0 - low
    values = coeffs[:, 0:rows]
    stacked = jnp.concatenate([values * mask for mask in (low, low * sign, high, high * sign)], axis=0)
    stacked = stacked.astype(bf16)
    main = rows - 1
    sums = jnp.dot(stacked[:, 0:main], leg_ref[0, 0:main, :], preferred_element_type=f32)
    last = stacked[:, main:rows].astype(f32) * leg_ref[0, main:rows, :].astype(f32)
    sums = sums + last
    for half in range(2):
        for side in range(2):
            at = (2 * half + side) * ROWS
            out_ref[half, :, 128 * side : 128 * side + 128] = sums[at : at + ROWS, :]


def legendre_sums(wave_pairs, spectral, legendre):
    slots, rows, northern = legendre.shape
    fields = spectral.shape[3]
    parts = jnp.transpose(spectral, (0, 3, 2, 1))
    return pl.pallas_call(
        functools.partial(legendre_kernel, rows - 2),
        out_shape=jax.ShapeDtypeStruct((2 * slots, ROWS, 2 * northern), f32),
        grid_spec=pltpu.PrefetchScalarGridSpec(
            num_scalar_prefetch=1,
            grid=(slots,),
            in_specs=[
                pl.BlockSpec((1, fields, 2, rows), lambda p, w: (p, 0, 0, 0)),
                pl.BlockSpec((1, rows, northern), lambda p, w: (p, 0, 0)),
            ],
            out_specs=pl.BlockSpec((2, ROWS, 2 * northern), lambda p, w: (p, 0, 0)),
            scratch_shapes=[pltpu.VMEM((ROWS, 1408), f32)],
        ),
    )(wave_pairs, parts, legendre)


def order_kernel(index_ref, sums_ref, out_ref, scratch):
    devices, lats = index_ref.shape[0], sums_ref.shape[2]
    lane = lax.broadcasted_iota(i32, (devices, lats), 1).astype(f32)
    onehot = jnp.concatenate(
        [jnp.where(index_ref[:, 10 + j : 11 + j] == lane, 1.0, 0.0) for j in range(4)], axis=0
    ).astype(bf16)
    for t in range(TILES):
        part = sums_ref[GROUPS * t : GROUPS * (t + 1)].reshape(GROUPS * ROWS, lats)
        part = jnp.concatenate([part, jnp.zeros((128 - GROUPS * ROWS, lats), f32)], axis=0).astype(bf16)
        picked = lax.dot_general(onehot, part, (((1,), (1,)), ((), ())), preferred_element_type=f32)
        for j in range(4):
            scratch[pl.ds(j * TILES + t, devices, 4 * TILES), :] = picked[devices * j : devices * (j + 1), :]
    out_ref[...] = scratch[...].reshape(out_ref.shape).astype(bf16)


def order_latitudes(index, sums):
    devices = index.shape[0]
    return pl.pallas_call(
        order_kernel,
        out_shape=jax.ShapeDtypeStruct((devices, 4 * TILES, 128), bf16),
        in_specs=[pl.BlockSpec(memory_space=pltpu.VMEM)] * 2,
        out_specs=pl.BlockSpec(memory_space=pltpu.VMEM),
        scratch_shapes=[pltpu.VMEM((devices * 4 * TILES, 128), f32)],
    )(index, sums)


def poly(coefficients, y):
    total = jnp.full_like(y, coefficients[-1])
    for c in coefficients[-2::-1]:
        total = total * y + c
    return total


def lat_scalars(lat_rows, npoints, l):
    points = npoints[lat_rows[l]]
    quarter = lax.shift_right_arithmetic(points, 2)
    chunks = lax.shift_right_arithmetic(quarter + (CHUNK - 1), 8)
    return points, quarter, chunks


BLOCK = 32


def table_kernel(truncation, lat_rows, npoints, index_ref, out_ref, waves):
    group = pl.program_id(0)
    devices = index_ref.shape[0]
    for g in range(GROUPS):

        @pl.when(group == g)
        def _():
            for t in range(TILES):
                ph = GROUPS * t + g
                column = index_ref[:, ph // 2 : ph // 2 + 1]
                if ph % 2:
                    column = truncation - column
                waves[devices * t : devices * (t + 1), :] = jnp.broadcast_to(column, (devices, 128))

    lane = lax.broadcasted_iota(i32, (BLOCK, 128), 1).astype(f32)
    first = [0, None, PAIR_CHUNKS, None]
    points, counts = [], []
    for l in range(4):
        n, _, count = lat_scalars(lat_rows, npoints, l)
        points.append(n)
        counts.append(count)
    first[1] = counts[0]
    first[3] = PAIR_CHUNKS + counts[2]

    def rows_block(r, carry):
        at = pl.multiple_of(r * BLOCK, BLOCK)
        k = waves[pl.ds(at, BLOCK), :]
        product = k * lane
        weight = jnp.where(k == 0.0, 1.0, 2.0)
        for l in range(4):
            n = jnp.full((BLOCK, 128), points[l], i32).astype(f32)
            inverse = 1.0 / n
            turns = jnp.floor(product * inverse + 0.5)
            f = (product - turns * n) * inverse
            y = f * f
            real = poly(COS, y)
            imag = poly(SIN, y) * f
            c64 = jnp.broadcast_to(real[:, 64:65], (BLOCK, 128))
            s64 = jnp.broadcast_to(imag[:, 64:65], (BLOCK, 128))
            c128 = 2.0 * c64 * c64 - 1.0
            s128 = 2.0 * c64 * s64
            scale = jnp.where(2.0 * k < n, weight, 0.0)
            real = real * scale
            imag = imag * (-scale)
            step = 2.0 * c128
            real_before = real * c128 - imag * s128
            imag_before = imag * c128 + real * s128

            def chunk(c, state):
                ra, ia, rb, ib = state
                rc = step * rb - ra
                ic = step * ib - ia
                to = first[l] + c
                out_ref[to, 0, pl.ds(at, BLOCK), 0:128] = rb.astype(bf16)
                out_ref[to, 0, pl.ds(at, BLOCK), 128:256] = rc.astype(bf16)
                out_ref[to, 1, pl.ds(at, BLOCK), 0:128] = ib.astype(bf16)
                out_ref[to, 1, pl.ds(at, BLOCK), 128:256] = ic.astype(bf16)
                return rc, ic, step * rc - rb, step * ic - ib

            lax.fori_loop(0, counts[l], chunk, (real_before, imag_before, real, imag))
        return carry

    lax.fori_loop(0, TILES * devices // BLOCK, rows_block, 0)


def fourier_tables(lat_rows, npoints, index, truncation):
    devices = index.shape[0]
    rows = TILES * devices
    return pl.pallas_call(
        functools.partial(table_kernel, float(truncation)),
        out_shape=jax.ShapeDtypeStruct((2 * PAIR_CHUNKS, 2, GROUPS * rows, CHUNK), bf16),
        grid_spec=pltpu.PrefetchScalarGridSpec(
            num_scalar_prefetch=2,
            grid=(GROUPS,),
            in_specs=[pl.BlockSpec((devices, 128), lambda g, a, b: (0, 0))],
            out_specs=pl.BlockSpec((2 * PAIR_CHUNKS, 2, rows, CHUNK), lambda g, a, b: (0, 0, g, 0)),
            scratch_shapes=[pltpu.VMEM((rows, 128), f32)],
        ),
        compiler_params=pltpu.CompilerParams(vmem_limit_bytes=32 << 20),
    )(lat_rows, npoints, index)


def synthesis_kernel(truncation, lat_rows, npoints, got_ref, wave_ref, select_ref, table_ref, out_ref, got, left, right, line):
    pair, step = pl.program_id(0), pl.program_id(1)
    devices = got_ref.shape[0]
    rows = TILES * devices

    @pl.when((pair == 0) & (step == 0))
    def _():
        got[...] = got_ref[...].reshape(devices * 4 * TILES, 128).astype(f32)
        line[...] = jnp.zeros_like(line)
        for l in range(4):
            stacked = jnp.concatenate(
                [got[pl.ds(l * TILES + t, devices, 4 * TILES), :] for t in range(TILES)], axis=0
            ).astype(bf16)
            both = lax.dot_general(select_ref[...], stacked, (((1,), (1,)), ((), ())), preferred_element_type=f32)
            for g in range(GROUPS):
                k = wave_ref[:, g * rows : (g + 1) * rows]
                row = lax.broadcasted_iota(i32, (ROWS, rows), 0)
                scale = jnp.where(row < 10, 1.0, jnp.broadcast_to(k / truncation, (ROWS, rows)))
                at = 2 * ROWS * g
                real = (both[at : at + ROWS] * scale).astype(bf16).astype(f32)
                imag = (both[at + ROWS : at + 2 * ROWS] * scale).astype(bf16).astype(f32)
                for a in range(4):
                    turn = a * k
                    turn = turn - 4.0 * jnp.floor(turn * 0.25)
                    cr = jnp.where(turn == 0.0, 1.0, jnp.where(turn == 2.0, -1.0, 0.0))
                    ci = jnp.where(turn == 1.0, 1.0, jnp.where(turn == 3.0, -1.0, 0.0))
                    left[l, a * ROWS : (a + 1) * ROWS, g * rows : (g + 1) * rows] = (real * cr - imag * ci).astype(bf16)
                    right[l, a * ROWS : (a + 1) * ROWS, g * rows : (g + 1) * rows] = (imag * cr + real * ci).astype(bf16)

    n_a, m_a, count_a = lat_scalars(lat_rows, npoints, 2 * pair)
    _, m_b, count_b = lat_scalars(lat_rows, npoints, 2 * pair + 1)
    second = step >= count_a
    l = 2 * pair + jnp.where(second, 1, 0)
    c = jnp.where(second, step - count_a, step)
    m = jnp.where(second, m_b, m_a)
    base = jnp.where(second, n_a, 0) + CHUNK * c
    length = m - CHUNK * c

    @pl.when(step < count_a + count_b)
    def _():
        values = jnp.dot(left[l], table_ref[0, 0], preferred_element_type=f32)
        values = values + jnp.dot(right[l], table_ref[0, 1], preferred_element_type=f32)
        lane = lax.broadcasted_iota(i32, (ROWS, 128), 1)
        for a in range(4):
            off = base + a * m
            tile = lax.shift_right_arithmetic(off, 7)
            shift = off & 127
            v0 = pltpu.roll(values[a * ROWS : (a + 1) * ROWS, 0:128], shift, 1)
            v1 = pltpu.roll(values[a * ROWS : (a + 1) * ROWS, 128:256], shift, 1)
            after = lane >= shift
            at = lane - shift
            line[tile] = jnp.where(after & (at < length), v0, line[tile])
            line[tile + 1] = jnp.where(at + 128 < length, jnp.where(after, v1, v0), line[tile + 1])
            line[tile + 2] = jnp.where(jnp.logical_not(after) & (at + 256 < length), v1, line[tile + 2])

    @pl.when(step == PAIR_CHUNKS - 1)
    def _():
        lane = lax.broadcasted_iota(i32, (ROWS, 128), 1)
        for q in range(4):
            shift = (QUARTER * q) % 128
            for i in range(QUARTER // 128 + 1):
                tile = QUARTER * q // 128 + i
                v = line[tile]
                if shift:
                    v = jnp.where(
                        lane < 128 - shift,
                        pltpu.roll(v, 128 - shift, 1),
                        pltpu.roll(line[tile + 1], 128 - shift, 1),
                    )
                width = min(128, QUARTER - 128 * i)
                out_ref[q, :, 128 * i : 128 * i + width] = v[0 : out_ref.shape[1], 0:width].astype(bf16)


def select_rows():
    table = np.zeros((GROUPS, 2 * ROWS, 128), np.float32)
    for g in range(GROUPS):
        for f in range(10):
            real, imag = g * ROWS + 2 * f, g * ROWS + 2 * f + 1
            table[g, f, real] = 1.0
            table[g, 10 + f, imag] = -1.0
            table[g, ROWS + f, imag] = 1.0
            table[g, ROWS + 10 + f, real] = 1.0
    return table.reshape(GROUPS * 2 * ROWS, 128).astype(jnp.bfloat16)


def synthesis(lat_rows, npoints, received, wave_line, tables, truncation):
    devices = received.shape[0]
    depth = GROUPS * TILES * devices

    def table_at(pair, step, lats, points):
        total = lat_scalars(lats, points, 2 * pair)[2] + lat_scalars(lats, points, 2 * pair + 1)[2]
        return (pair * PAIR_CHUNKS + jnp.minimum(step, total - 1), 0, 0, 0)

    return pl.pallas_call(
        functools.partial(synthesis_kernel, float(truncation)),
        out_shape=jax.ShapeDtypeStruct((8, 20, QUARTER), bf16),
        grid_spec=pltpu.PrefetchScalarGridSpec(
            num_scalar_prefetch=2,
            grid=(2, PAIR_CHUNKS),
            in_specs=[
                pl.BlockSpec((devices, 4 * TILES, 128), lambda p, s, a, b: (0, 0, 0)),
                pl.BlockSpec((1, depth), lambda p, s, a, b: (0, 0)),
                pl.BlockSpec((GROUPS * 2 * ROWS, 128), lambda p, s, a, b: (0, 0)),
                pl.BlockSpec((1, 2, depth, CHUNK), table_at),
            ],
            out_specs=pl.BlockSpec((4, 20, QUARTER), lambda p, s, a, b: (p, 0, 0)),
            scratch_shapes=[
                pltpu.VMEM((devices * 4 * TILES, 128), f32),
                pltpu.VMEM((4, 4 * ROWS, depth), bf16),
                pltpu.VMEM((4, 4 * ROWS, depth), bf16),
                pltpu.VMEM((44, ROWS, 128), f32),
            ],
        ),
        compiler_params=pltpu.CompilerParams(vmem_limit_bytes=32 << 20),
    )(lat_rows, npoints, received, wave_line, select_rows(), tables)


def wave_line_of(index, truncation):
    low = jnp.transpose(index[:, 0:10])
    both = jnp.stack([low, truncation - low], axis=1)
    both = both.reshape(TILES, GROUPS, index.shape[0])
    return jnp.transpose(both, (1, 0, 2)).reshape(1, -1)


def on_device(spectral, legendre, wave_pairs, npoints, lat_rows):
    truncation = legendre.shape[1] - 2
    devices = lax.axis_size("wave")
    mine = jnp.concatenate([wave_pairs, lat_rows]).astype(f32)
    mine = jnp.pad(mine, (0, 128 - mine.shape[0]))
    index = lax.all_to_all(jnp.broadcast_to(mine[None, None, :], (devices, 1, 128)), "wave", 0, 0, tiled=True)
    index = index.reshape(devices, 128)
    sums = legendre_sums(wave_pairs, spectral, legendre)
    ordered = order_latitudes(index, sums)
    received = lax.all_to_all(ordered, "wave", 0, 0, tiled=True)
    tables = fourier_tables(lat_rows, npoints, index, truncation)
    wave_line = wave_line_of(index, float(truncation))
    blocks = synthesis(lat_rows, npoints, received, wave_line, tables, truncation)
    blocks = lax.all_to_all(blocks, "field", 0, 0, tiled=True)
    blocks = blocks.reshape(8, 2, 10, QUARTER)
    return jnp.transpose(blocks, (1, 0, 2, 3)).reshape(2, 80, QUARTER)


def solution(mesh):
    placed = (P("wave", None, None, "field"), P("wave", None, None), P("wave"), P(), P("wave"))
    return jax.shard_map(
        on_device,
        mesh=mesh,
        in_specs=placed,
        out_specs=P(None, None, ("wave", "field")),
        check_vma=False,
    )
```

```python
import functools

import jax
import jax.numpy as jnp
import numpy as np
from jax import lax
from jax.experimental import pallas as pl
from jax.experimental.pallas import tpu as pltpu
from jax.sharding import PartitionSpec as P

ROW_PAIR = 5156
QUARTER = ROW_PAIR // 4
CHUNK = 256
GROUPS = 5
TILES = 4
ROWS = 24
SIN = (6.283184905907144, -41.34158660945749, 81.59984497508991, -76.61321302879018, 41.33641025544816, -12.459753683550199)
COS = (0.999999988711474, -19.739204378854772, 64.93911099976975, -85.4500154366872, 60.16656814312298, -25.963448256110482, 6.5226306139218035)
f32, bf16, i32 = jnp.float32, jnp.bfloat16, jnp.int32


def legendre_kernel(truncation, waves, spec_ref, leg_ref, out_ref, coeffs):
    slot = pl.program_id(0)
    rows = truncation + 2
    fields = spec_ref.shape[1]

    @pl.when(slot == 0)
    def _():
        coeffs[...] = jnp.zeros_like(coeffs)

    for field in range(fields):
        coeffs[2 * field : 2 * field + 2, 0:rows] = spec_ref[0, field]
    split = truncation + 1 - waves[slot]
    row = lax.broadcasted_iota(i32, (1, rows), 1)
    low = row < split
    offset = jnp.where(low, row, row - split)
    sign = jnp.where(offset % 2 == 0, 1.0, -1.0).astype(f32)
    low = jnp.where(low, 1.0, 0.0).astype(f32)
    high = 1.0 - low
    values = coeffs[:, 0:rows]
    stacked = jnp.concatenate([values * mask for mask in (low, low * sign, high, high * sign)], axis=0)
    stacked = stacked.astype(bf16)
    main = rows - 1
    sums = jnp.dot(stacked[:, 0:main], leg_ref[0, 0:main, :], preferred_element_type=f32)
    last = stacked[:, main:rows].astype(f32) * leg_ref[0, main:rows, :].astype(f32)
    sums = sums + last
    for half in range(2):
        for side in range(2):
            at = (2 * half + side) * ROWS
            out_ref[half, :, 128 * side : 128 * side + 128] = sums[at : at + ROWS, :]


def legendre_sums(wave_pairs, spectral, legendre):
    slots, rows, northern = legendre.shape
    fields = spectral.shape[3]
    parts = jnp.transpose(spectral, (0, 3, 2, 1))
    return pl.pallas_call(
        functools.partial(legendre_kernel, rows - 2),
        out_shape=jax.ShapeDtypeStruct((2 * slots, ROWS, 2 * northern), f32),
        grid_spec=pltpu.PrefetchScalarGridSpec(
            num_scalar_prefetch=1,
            grid=(slots,),
            in_specs=[
                pl.BlockSpec((1, fields, 2, rows), lambda p, w: (p, 0, 0, 0)),
                pl.BlockSpec((1, rows, northern), lambda p, w: (p, 0, 0)),
            ],
            out_specs=pl.BlockSpec((2, ROWS, 2 * northern), lambda p, w: (p, 0, 0)),
            scratch_shapes=[pltpu.VMEM((ROWS, 1408), f32)],
        ),
    )(wave_pairs, parts, legendre)


def order_kernel(index_ref, sums_ref, out_ref, scratch):
    devices, lats = index_ref.shape[0], sums_ref.shape[2]
    lane = lax.broadcasted_iota(i32, (devices, lats), 1).astype(f32)
    onehot = jnp.concatenate(
        [jnp.where(index_ref[:, 10 + j : 11 + j] == lane, 1.0, 0.0) for j in range(4)], axis=0
    ).astype(bf16)
    for t in range(TILES):
        part = sums_ref[GROUPS * t : GROUPS * (t + 1)].reshape(GROUPS * ROWS, lats)
        part = jnp.concatenate([part, jnp.zeros((128 - GROUPS * ROWS, lats), f32)], axis=0).astype(bf16)
        picked = lax.dot_general(onehot, part, (((1,), (1,)), ((), ())), preferred_element_type=f32)
        for j in range(4):
            scratch[pl.ds(j * TILES + t, devices, 4 * TILES), :] = picked[devices * j : devices * (j + 1), :]
    out_ref[...] = scratch[...].reshape(out_ref.shape).astype(bf16)


def order_latitudes(index, sums):
    devices = index.shape[0]
    return pl.pallas_call(
        order_kernel,
        out_shape=jax.ShapeDtypeStruct((devices, 4 * TILES, 128), bf16),
        in_specs=[pl.BlockSpec(memory_space=pltpu.VMEM)] * 2,
        out_specs=pl.BlockSpec(memory_space=pltpu.VMEM),
        scratch_shapes=[pltpu.VMEM((devices * 4 * TILES, 128), f32)],
    )(index, sums)


def poly(coefficients, y):
    total = jnp.full_like(y, coefficients[-1])
    for c in coefficients[-2::-1]:
        total = total * y + c
    return total


def sincos(product, n, inverse):
    turns = jnp.floor(product * inverse + 0.5)
    f = (product - turns * n) * inverse
    y = f * f
    return poly(COS, y), poly(SIN, y) * f


BLOCK = 64


def table_kernel(truncation, lat_rows, npoints, index_ref, out_ref, waves):
    l = pl.program_id(0)
    devices = index_ref.shape[0]
    depth = GROUPS * TILES * devices

    @pl.when(l == 0)
    def _():
        for g in range(GROUPS):
            for t in range(TILES):
                ph = GROUPS * t + g
                column = index_ref[:, ph // 2 : ph // 2 + 1]
                if ph % 2:
                    column = truncation - column
                at = devices * (TILES * g + t)
                waves[at : at + devices, :] = jnp.broadcast_to(column, (devices, 128))

    lane = lax.broadcasted_iota(i32, (BLOCK, 128), 1).astype(f32)
    n = jnp.full((8, 128), npoints[lat_rows[l]], i32).astype(f32)
    inverse = 1.0 / n
    n, inverse = n[0:1], inverse[0:1]

    def rows_block(r, carry):
        at = pl.multiple_of(r * BLOCK, BLOCK)
        k = waves[pl.ds(at, BLOCK), :]
        real, imag = sincos(k * lane, n, inverse)
        c64 = jnp.broadcast_to(real[:, 64:65], (BLOCK, 128))
        s64 = jnp.broadcast_to(imag[:, 64:65], (BLOCK, 128))
        c128 = 2.0 * c64 * c64 - 1.0
        s128 = 2.0 * c64 * s64
        scale = jnp.where(2.0 * k < n, jnp.where(k == 0.0, 1.0, 2.0), 0.0)
        real = real * scale
        imag = imag * scale
        out_ref[0, pl.ds(at, BLOCK), 0:128] = real.astype(bf16)
        out_ref[0, pl.ds(at, BLOCK), 128:256] = (real * c128 - imag * s128).astype(bf16)
        out_ref[0, pl.ds(depth + at, BLOCK), 0:128] = (-imag).astype(bf16)
        out_ref[0, pl.ds(depth + at, BLOCK), 128:256] = (-imag * c128 - real * s128).astype(bf16)
        return carry

    lax.fori_loop(0, depth // BLOCK, rows_block, 0)


def fourier_tables(lat_rows, npoints, index, truncation):
    devices = index.shape[0]
    depth = GROUPS * TILES * devices
    return pl.pallas_call(
        functools.partial(table_kernel, float(truncation)),
        out_shape=jax.ShapeDtypeStruct((4, 2 * depth, CHUNK), bf16),
        grid_spec=pltpu.PrefetchScalarGridSpec(
            num_scalar_prefetch=2,
            grid=(4,),
            in_specs=[pl.BlockSpec((devices, 128), lambda l, a, b: (0, 0))],
            out_specs=pl.BlockSpec((1, 2 * depth, CHUNK), lambda l, a, b: (l, 0, 0)),
            scratch_shapes=[pltpu.VMEM((depth, 128), f32)],
        ),
    )(lat_rows, npoints, index)


BATCH = 8
STEPS = 4
LAST = ROW_PAIR // CHUNK


def pair_batches(lat_rows, npoints, pair):
    n_a = npoints[lat_rows[2 * pair]]
    start_b = lax.shift_right_arithmetic(n_a, 8)
    batches_a = lax.shift_right_arithmetic(lax.shift_right_arithmetic(n_a - 1, 8) + BATCH, 3)
    batches_b = lax.shift_right_arithmetic(LAST - start_b + BATCH, 3)
    return n_a, start_b, batches_a, batches_a + batches_b


def synthesis_kernel(truncation, lat_rows, npoints, got_ref, wave_ref, select_ref, table_ref, out_ref, got, parts, left, line):
    pair, step = pl.program_id(0), pl.program_id(1)
    devices = got_ref.shape[0]
    rows = TILES * devices
    depth = GROUPS * rows

    @pl.when((pair == 0) & (step == 0))
    def _():
        got[...] = got_ref[...].reshape(devices * 4 * TILES, 128).astype(f32)
        for l in range(4):
            stacked = jnp.concatenate(
                [got[pl.ds(l * TILES + t, devices, 4 * TILES), :] for t in range(TILES)], axis=0
            ).astype(bf16)
            both = lax.dot_general(select_ref[...], stacked, (((1,), (1,)), ((), ())), preferred_element_type=f32)
            for g in range(GROUPS):
                k = wave_ref[:, g * rows : (g + 1) * rows]
                row = lax.broadcasted_iota(i32, (ROWS, rows), 0)
                scale = jnp.where(row < 10, 1.0, jnp.broadcast_to(k / truncation, (ROWS, rows)))
                at = 2 * ROWS * g
                for c in range(2):
                    part = both[at + c * ROWS : at + (c + 1) * ROWS] * scale
                    parts[l, c, :, g * rows : (g + 1) * rows] = part.astype(bf16).astype(f32)

    n_a, start_b, batches_a, batches = pair_batches(lat_rows, npoints, pair)
    second = step >= batches_a
    l = 2 * pair + jnp.where(second, 1, 0)
    first = jnp.where(second, start_b + BATCH * (step - batches_a), BATCH * step)
    origin = jnp.where(second, n_a, 0)

    @pl.when(step < batches)
    def _():
        n = jnp.full((8, 128), npoints[lat_rows[l]], i32).astype(f32)
        inverse = (1.0 / n)[0:1, 0:1]
        n = n[0:1, 0:1]
        chunk = lax.broadcasted_iota(i32, (BATCH, rows), 0)
        t0 = ((first + chunk) * CHUNK - origin).astype(f32)
        for g in range(GROUPS):
            at = slice(g * rows, (g + 1) * rows)
            k = wave_ref[:, at]
            cosine, sine = sincos(t0 * k, n, inverse)
            real, imag = parts[l, 0, :, at], parts[l, 1, :, at]
            for j in range(0, BATCH, 2):
                turned = [
                    (real * cosine[i : i + 1] - imag * sine[i : i + 1], imag * cosine[i : i + 1] + real * sine[i : i + 1])
                    for i in (j, j + 1)
                ]
                to = slice(j * ROWS, (j + 2) * ROWS)
                left[to, at] = jnp.concatenate([turned[0][0], turned[1][0]], axis=0).astype(bf16)
                at_imag = slice(depth + g * rows, depth + (g + 1) * rows)
                left[to, at_imag] = jnp.concatenate([turned[0][1], turned[1][1]], axis=0).astype(bf16)
        values = jnp.dot(left[...], table_ref[0], preferred_element_type=f32)
        lane = lax.broadcasted_iota(i32, (ROWS, 128), 1)
        for j in range(BATCH):
            for half in range(2):
                tile = 2 * (first + j) + half
                mine = lane + tile * 128 >= origin
                new = values[j * ROWS : (j + 1) * ROWS, 128 * half : 128 * half + 128]
                line[tile] = jnp.where(mine, new, line[tile])

    @pl.when(step == STEPS - 1)
    def _():
        lane = lax.broadcasted_iota(i32, (ROWS, 128), 1)
        for q in range(4):
            shift = (QUARTER * q) % 128
            for i in range(QUARTER // 128 + 1):
                tile = QUARTER * q // 128 + i
                v = line[tile]
                if shift:
                    v = jnp.where(
                        lane < 128 - shift,
                        pltpu.roll(v, 128 - shift, 1),
                        pltpu.roll(line[tile + 1], 128 - shift, 1),
                    )
                width = min(128, QUARTER - 128 * i)
                out_ref[q, :, 128 * i : 128 * i + width] = v[0 : out_ref.shape[1], 0:width].astype(bf16)


def select_rows():
    table = np.zeros((GROUPS, 2 * ROWS, 128), np.float32)
    for g in range(GROUPS):
        for f in range(10):
            real, imag = g * ROWS + 2 * f, g * ROWS + 2 * f + 1
            table[g, f, real] = 1.0
            table[g, 10 + f, imag] = -1.0
            table[g, ROWS + f, imag] = 1.0
            table[g, ROWS + 10 + f, real] = 1.0
    return table.reshape(GROUPS * 2 * ROWS, 128).astype(jnp.bfloat16)


def synthesis(lat_rows, npoints, received, wave_line, tables, truncation):
    devices = received.shape[0]
    depth = GROUPS * TILES * devices

    def table_at(pair, step, lats, points):
        _, _, batches_a, batches = pair_batches(lats, points, pair)
        return (2 * pair + jnp.where(jnp.minimum(step, batches - 1) >= batches_a, 1, 0), 0, 0)

    return pl.pallas_call(
        functools.partial(synthesis_kernel, float(truncation)),
        out_shape=jax.ShapeDtypeStruct((8, 20, QUARTER), bf16),
        grid_spec=pltpu.PrefetchScalarGridSpec(
            num_scalar_prefetch=2,
            grid=(2, STEPS),
            in_specs=[
                pl.BlockSpec((devices, 4 * TILES, 128), lambda p, s, a, b: (0, 0, 0)),
                pl.BlockSpec((1, depth), lambda p, s, a, b: (0, 0)),
                pl.BlockSpec((GROUPS * 2 * ROWS, 128), lambda p, s, a, b: (0, 0)),
                pl.BlockSpec((1, 2 * depth, CHUNK), table_at),
            ],
            out_specs=pl.BlockSpec((4, 20, QUARTER), lambda p, s, a, b: (p, 0, 0)),
            scratch_shapes=[
                pltpu.VMEM((devices * 4 * TILES, 128), f32),
                pltpu.VMEM((4, 2, ROWS, depth), f32),
                pltpu.VMEM((BATCH * ROWS, 2 * depth), bf16),
                pltpu.VMEM((2 * (LAST + BATCH) + 2, ROWS, 128), f32),
            ],
        ),
        compiler_params=pltpu.CompilerParams(vmem_limit_bytes=32 << 20),
    )(lat_rows, npoints, received, wave_line, select_rows(), tables)


def wave_line_of(index, truncation):
    low = jnp.transpose(index[:, 0:10])
    both = jnp.stack([low, truncation - low], axis=1)
    both = both.reshape(TILES, GROUPS, index.shape[0])
    return jnp.transpose(both, (1, 0, 2)).reshape(1, -1)


def on_device(spectral, legendre, wave_pairs, npoints, lat_rows):
    truncation = legendre.shape[1] - 2
    devices = lax.axis_size("wave")
    mine = jnp.concatenate([wave_pairs, lat_rows]).astype(f32)
    mine = jnp.pad(mine, (0, 128 - mine.shape[0]))
    index = lax.all_to_all(jnp.broadcast_to(mine[None, None, :], (devices, 1, 128)), "wave", 0, 0, tiled=True)
    index = index.reshape(devices, 128)
    sums = legendre_sums(wave_pairs, spectral, legendre)
    ordered = order_latitudes(index, sums)
    received = lax.all_to_all(ordered, "wave", 0, 0, tiled=True)
    tables = fourier_tables(lat_rows, npoints, index, truncation)
    wave_line = wave_line_of(index, float(truncation))
    blocks = synthesis(lat_rows, npoints, received, wave_line, tables, truncation)
    blocks = lax.all_to_all(blocks, "field", 0, 0, tiled=True)
    blocks = blocks.reshape(8, 2, 10, QUARTER)
    return jnp.transpose(blocks, (1, 0, 2, 3)).reshape(2, 80, QUARTER)


def solution(mesh):
    placed = (P("wave", None, None, "field"), P("wave", None, None), P("wave"), P(), P("wave"))
    return jax.shard_map(
        on_device,
        mesh=mesh,
        in_specs=placed,
        out_specs=P(None, None, ("wave", "field")),
        check_vma=False,
    )
```

```python
import functools

import jax
import jax.numpy as jnp
import numpy as np
from jax import lax
from jax.experimental import pallas as pl
from jax.experimental.pallas import tpu as pltpu
from jax.sharding import PartitionSpec as P

ROW_PAIR = 5156
QUARTER = ROW_PAIR // 4
CHUNK = 256
GROUPS = 5
TILES = 4
ROWS = 24
SIN = (6.283184915155849, -41.3415888250942, 81.59992747560547, -76.6142661520567, 41.34181133252104, -12.469328879159221)
COS = (0.9999992080920543, -19.73897953618229, 64.92862553583919, -85.27120644254374, 58.78833787867872, -21.067254412050286)
f32, bf16, i32 = jnp.float32, jnp.bfloat16, jnp.int32


def legendre_kernel(truncation, waves, spec_ref, leg_ref, out_ref, coeffs):
    slot = pl.program_id(0)
    rows = truncation + 2
    fields = spec_ref.shape[1]

    @pl.when(slot == 0)
    def _():
        coeffs[...] = jnp.zeros_like(coeffs)

    for field in range(fields):
        coeffs[2 * field : 2 * field + 2, 0:rows] = spec_ref[0, field]
    split = truncation + 1 - waves[slot]
    row = lax.broadcasted_iota(i32, (1, rows), 1)
    low = row < split
    offset = jnp.where(low, row, row - split)
    sign = jnp.where(offset % 2 == 0, 1.0, -1.0).astype(f32)
    low = jnp.where(low, 1.0, 0.0).astype(f32)
    high = 1.0 - low
    values = coeffs[:, 0:rows]
    stacked = jnp.concatenate([values * mask for mask in (low, low * sign, high, high * sign)], axis=0)
    stacked = stacked.astype(bf16)
    main = rows - 1
    sums = jnp.dot(stacked[:, 0:main], leg_ref[0, 0:main, :], preferred_element_type=f32)
    last = stacked[:, main:rows].astype(f32) * leg_ref[0, main:rows, :].astype(f32)
    sums = sums + last
    for half in range(2):
        for side in range(2):
            at = (2 * half + side) * ROWS
            out_ref[half, :, 128 * side : 128 * side + 128] = sums[at : at + ROWS, :]


def legendre_sums(wave_pairs, spectral, legendre):
    slots, rows, northern = legendre.shape
    fields = spectral.shape[3]
    parts = jnp.transpose(spectral, (0, 3, 2, 1))
    return pl.pallas_call(
        functools.partial(legendre_kernel, rows - 2),
        out_shape=jax.ShapeDtypeStruct((2 * slots, ROWS, 2 * northern), f32),
        grid_spec=pltpu.PrefetchScalarGridSpec(
            num_scalar_prefetch=1,
            grid=(slots,),
            in_specs=[
                pl.BlockSpec((1, fields, 2, rows), lambda p, w: (p, 0, 0, 0)),
                pl.BlockSpec((1, rows, northern), lambda p, w: (p, 0, 0)),
            ],
            out_specs=pl.BlockSpec((2, ROWS, 2 * northern), lambda p, w: (p, 0, 0)),
            scratch_shapes=[pltpu.VMEM((ROWS, 1408), f32)],
        ),
    )(wave_pairs, parts, legendre)


def order_kernel(index_ref, sums_ref, out_ref, scratch):
    devices, lats = index_ref.shape[0], sums_ref.shape[2]
    lane = lax.broadcasted_iota(i32, (devices, lats), 1).astype(f32)
    onehot = jnp.concatenate(
        [jnp.where(index_ref[:, 10 + j : 11 + j] == lane, 1.0, 0.0) for j in range(4)], axis=0
    ).astype(bf16)
    for t in range(TILES):
        part = sums_ref[GROUPS * t : GROUPS * (t + 1)].reshape(GROUPS * ROWS, lats)
        part = jnp.concatenate([part, jnp.zeros((128 - GROUPS * ROWS, lats), f32)], axis=0).astype(bf16)
        picked = lax.dot_general(onehot, part, (((1,), (1,)), ((), ())), preferred_element_type=f32)
        for j in range(4):
            scratch[pl.ds(j * TILES + t, devices, 4 * TILES), :] = picked[devices * j : devices * (j + 1), :]
    out_ref[...] = scratch[...].reshape(out_ref.shape).astype(bf16)


def order_latitudes(index, sums):
    devices = index.shape[0]
    return pl.pallas_call(
        order_kernel,
        out_shape=jax.ShapeDtypeStruct((devices, 4 * TILES, 128), bf16),
        grid=(1,),
        in_specs=[pl.BlockSpec(index.shape, lambda i: (0, 0)), pl.BlockSpec(sums.shape, lambda i: (0, 0, 0))],
        out_specs=pl.BlockSpec((devices, 4 * TILES, 128), lambda i: (0, 0, 0)),
        scratch_shapes=[pltpu.VMEM((devices * 4 * TILES, 128), f32)],
    )(index, sums)


def poly(coefficients, y):
    total = jnp.full_like(y, coefficients[-1])
    for c in coefficients[-2::-1]:
        total = total * y + c
    return total


def sincos(product, n, inverse):
    turns = jnp.floor(product * inverse + 0.5)
    f = (product - turns * n) * inverse
    y = f * f
    return poly(COS, y), poly(SIN, y) * f


BLOCK = 128


def table_kernel(truncation, lat_rows, npoints, index_ref, out_ref, waves):
    l = pl.program_id(0)
    devices = index_ref.shape[0]
    depth = GROUPS * TILES * devices

    @pl.when(l == 0)
    def _():
        for g in range(GROUPS):
            for t in range(TILES):
                ph = GROUPS * t + g
                column = index_ref[:, ph // 2 : ph // 2 + 1]
                if ph % 2:
                    column = truncation - column
                at = devices * (TILES * g + t)
                waves[at : at + devices, :] = jnp.broadcast_to(column, (devices, 128))

    odd = (2 * lax.broadcasted_iota(i32, (BLOCK, 128), 1) + 1).astype(f32)
    n = jnp.full((8, 128), 2 * npoints[lat_rows[l]], i32).astype(f32)
    inverse = (1.0 / n)[0:1]
    n = n[0:1]

    def rows_block(r, carry):
        at = pl.multiple_of(r * BLOCK, BLOCK)
        cosine, sine = sincos(waves[pl.ds(at, BLOCK), :] * odd, n, inverse)
        out_ref[0, pl.ds(at, BLOCK), :] = cosine.astype(bf16)
        out_ref[0, pl.ds(depth + at, BLOCK), :] = sine.astype(bf16)
        return carry

    lax.fori_loop(0, depth // BLOCK, rows_block, 0)


def fourier_tables(lat_rows, npoints, index, truncation):
    devices = index.shape[0]
    depth = GROUPS * TILES * devices
    return pl.pallas_call(
        functools.partial(table_kernel, float(truncation)),
        out_shape=jax.ShapeDtypeStruct((4, 2 * depth, CHUNK // 2), bf16),
        grid_spec=pltpu.PrefetchScalarGridSpec(
            num_scalar_prefetch=2,
            grid=(4,),
            in_specs=[pl.BlockSpec((devices, 128), lambda l, a, b: (0, 0))],
            out_specs=pl.BlockSpec((1, 2 * depth, CHUNK // 2), lambda l, a, b: (l, 0, 0)),
            scratch_shapes=[pltpu.VMEM((depth, 128), f32)],
        ),
    )(lat_rows, npoints, index)


BATCH = 8
STEPS = 4
LAST = ROW_PAIR // CHUNK


def pair_batches(lat_rows, npoints, pair):
    n_a = npoints[lat_rows[2 * pair]]
    start_b = lax.shift_right_arithmetic(n_a, 8)
    batches_a = lax.shift_right_arithmetic(lax.shift_right_arithmetic(n_a - 1, 8) + BATCH, 3)
    batches_b = lax.shift_right_arithmetic(LAST - start_b + BATCH, 3)
    return n_a, start_b, batches_a, batches_a + batches_b


def synthesis_kernel(truncation, lat_rows, npoints, got_ref, wave_ref, select_ref, reverse_ref, table_ref, out_ref, got, parts, left, line):
    pair, step = pl.program_id(0), pl.program_id(1)
    devices = got_ref.shape[0]
    rows = TILES * devices
    depth = GROUPS * rows

    @pl.when((pair == 0) & (step == 0))
    def _():
        got[...] = got_ref[...].reshape(devices * 4 * TILES, 128).astype(f32)
        for l in range(4):
            stacked = jnp.concatenate(
                [got[pl.ds(l * TILES + t, devices, 4 * TILES), :] for t in range(TILES)], axis=0
            ).astype(bf16)
            both = lax.dot_general(select_ref[...], stacked, (((1,), (1,)), ((), ())), preferred_element_type=f32)
            for g in range(GROUPS):
                k = wave_ref[:, g * rows : (g + 1) * rows]
                row = lax.broadcasted_iota(i32, (ROWS, rows), 0)
                scale = jnp.where(row < 10, 1.0, jnp.broadcast_to(k / truncation, (ROWS, rows)))
                at = 2 * ROWS * g
                for c in range(2):
                    part = both[at + c * ROWS : at + (c + 1) * ROWS] * scale
                    parts[l, c, :, g * rows : (g + 1) * rows] = part.astype(bf16).astype(f32)

    n_a, start_b, batches_a, batches = pair_batches(lat_rows, npoints, pair)
    second = step >= batches_a
    l = 2 * pair + jnp.where(second, 1, 0)
    first = jnp.where(second, start_b + BATCH * (step - batches_a), BATCH * step)
    origin = jnp.where(second, n_a, 0)

    @pl.when(step < batches)
    def _():
        n = jnp.full((8, 128), 2 * npoints[lat_rows[l]], i32).astype(f32)
        inverse = (1.0 / n)[0:1, 0:1]
        n = n[0:1, 0:1]
        chunk = lax.broadcasted_iota(i32, (BATCH, rows), 0)
        center = (2 * CHUNK * (first + chunk) - 2 * origin + CHUNK - 1).astype(f32)
        for g in range(GROUPS):
            at = slice(g * rows, (g + 1) * rows)
            k = wave_ref[:, at]
            weight = jnp.where(4.0 * k < n, jnp.where(k == 0.0, 1.0, 2.0), 0.0)
            cosine, sine = sincos(center * k, n, inverse)
            cosine, sine = cosine * weight, sine * weight
            real, imag = parts[l, 0, :, at], parts[l, 1, :, at]
            for j in range(0, BATCH, 2):
                turned = [
                    (real * cosine[i : i + 1] - imag * sine[i : i + 1], imag * cosine[i : i + 1] + real * sine[i : i + 1])
                    for i in (j, j + 1)
                ]
                to = slice(j * ROWS, (j + 2) * ROWS)
                left[to, at] = jnp.concatenate([turned[0][0], turned[1][0]], axis=0).astype(bf16)
                at_imag = slice(depth + g * rows, depth + (g + 1) * rows)
                left[to, at_imag] = jnp.concatenate([turned[0][1], turned[1][1]], axis=0).astype(bf16)
        even = jnp.dot(left[:, 0:depth], table_ref[0, 0:depth], preferred_element_type=f32)
        odd = jnp.dot(left[:, depth : 2 * depth], table_ref[0, depth : 2 * depth], preferred_element_type=f32)
        before = jnp.dot((even + odd).astype(bf16), reverse_ref[...], preferred_element_type=f32)
        after = even - odd
        lane = lax.broadcasted_iota(i32, (ROWS, 128), 1)
        for j in range(BATCH):
            for half, values in ((0, before), (1, after)):
                tile = 2 * (first + j) + half
                mine = lane + tile * 128 >= origin
                line[tile] = jnp.where(mine, values[j * ROWS : (j + 1) * ROWS], line[tile])

    @pl.when(step == STEPS - 1)
    def _():
        lane = lax.broadcasted_iota(i32, (ROWS, 128), 1)
        for q in range(4):
            shift = (QUARTER * q) % 128
            for i in range(QUARTER // 128 + 1):
                tile = QUARTER * q // 128 + i
                v = line[tile]
                if shift:
                    v = jnp.where(
                        lane < 128 - shift,
                        pltpu.roll(v, 128 - shift, 1),
                        pltpu.roll(line[tile + 1], 128 - shift, 1),
                    )
                width = min(128, QUARTER - 128 * i)
                out_ref[q, :, 128 * i : 128 * i + width] = v[0 : out_ref.shape[1], 0:width].astype(bf16)


def select_rows():
    table = np.zeros((GROUPS, 2 * ROWS, 128), np.float32)
    for g in range(GROUPS):
        for f in range(10):
            real, imag = g * ROWS + 2 * f, g * ROWS + 2 * f + 1
            table[g, f, real] = 1.0
            table[g, 10 + f, imag] = -1.0
            table[g, ROWS + f, imag] = 1.0
            table[g, ROWS + 10 + f, real] = 1.0
    return table.reshape(GROUPS * 2 * ROWS, 128).astype(jnp.bfloat16)


def synthesis(lat_rows, npoints, received, wave_line, tables, truncation):
    devices = received.shape[0]
    depth = GROUPS * TILES * devices

    reverse = np.eye(128)[::-1].astype(jnp.bfloat16)

    def table_at(pair, step, lats, points):
        _, _, batches_a, batches = pair_batches(lats, points, pair)
        return (2 * pair + jnp.where(jnp.minimum(step, batches - 1) >= batches_a, 1, 0), 0, 0)

    return pl.pallas_call(
        functools.partial(synthesis_kernel, float(truncation)),
        out_shape=jax.ShapeDtypeStruct((8, 20, QUARTER), bf16),
        grid_spec=pltpu.PrefetchScalarGridSpec(
            num_scalar_prefetch=2,
            grid=(2, STEPS),
            in_specs=[
                pl.BlockSpec((devices, 4 * TILES, 128), lambda p, s, a, b: (0, 0, 0)),
                pl.BlockSpec((1, depth), lambda p, s, a, b: (0, 0)),
                pl.BlockSpec((GROUPS * 2 * ROWS, 128), lambda p, s, a, b: (0, 0)),
                pl.BlockSpec((128, 128), lambda p, s, a, b: (0, 0)),
                pl.BlockSpec((1, 2 * depth, CHUNK // 2), table_at),
            ],
            out_specs=pl.BlockSpec((4, 20, QUARTER), lambda p, s, a, b: (p, 0, 0)),
            scratch_shapes=[
                pltpu.VMEM((devices * 4 * TILES, 128), f32),
                pltpu.VMEM((4, 2, ROWS, depth), f32),
                pltpu.VMEM((BATCH * ROWS, 2 * depth), bf16),
                pltpu.VMEM((2 * (LAST + BATCH) + 2, ROWS, 128), f32),
            ],
        ),
        compiler_params=pltpu.CompilerParams(vmem_limit_bytes=32 << 20),
    )(lat_rows, npoints, received, wave_line, select_rows(), reverse, tables)


def wave_line_of(index, truncation):
    low = jnp.transpose(index[:, 0:10])
    both = jnp.stack([low, truncation - low], axis=1)
    both = both.reshape(TILES, GROUPS, index.shape[0])
    return jnp.transpose(both, (1, 0, 2)).reshape(1, -1)


def on_device(spectral, legendre, wave_pairs, npoints, lat_rows):
    truncation = legendre.shape[1] - 2
    devices = lax.axis_size("wave")
    mine = jnp.concatenate([wave_pairs, lat_rows]).astype(f32)
    mine = jnp.pad(mine, (0, 128 - mine.shape[0]))
    index = lax.all_to_all(jnp.broadcast_to(mine[None, None, :], (devices, 1, 128)), "wave", 0, 0, tiled=True)
    index = index.reshape(devices, 128)
    sums = legendre_sums(wave_pairs, spectral, legendre)
    ordered = order_latitudes(index, sums)
    received = lax.all_to_all(ordered, "wave", 0, 0, tiled=True)
    tables = fourier_tables(lat_rows, npoints, index, truncation)
    tables = pltpu.with_memory_space_constraint(tables, pltpu.HBM)
    wave_line = wave_line_of(index, float(truncation))
    blocks = synthesis(lat_rows, npoints, received, wave_line, tables, truncation)
    blocks = lax.all_to_all(blocks, "field", 0, 0, tiled=True)
    blocks = blocks.reshape(8, 2, 10, QUARTER)
    return jnp.transpose(blocks, (1, 0, 2, 3)).reshape(2, 80, QUARTER)


def solution(mesh):
    placed = (P("wave", None, None, "field"), P("wave", None, None), P("wave"), P(), P("wave"))
    return jax.shard_map(
        on_device,
        mesh=mesh,
        in_specs=placed,
        out_specs=P(None, None, ("wave", "field")),
        check_vma=False,
    )
```

```python
import functools

import jax
import jax.numpy as jnp
import numpy as np
from jax import lax
from jax.experimental import pallas as pl
from jax.experimental.pallas import tpu as pltpu
from jax.sharding import PartitionSpec as P

ROW_PAIR = 5156
QUARTER = ROW_PAIR // 4
CHUNK = 256
GROUPS = 5
TILES = 4
ROWS = 24
SIN = (6.283184915155849, -41.3415888250942, 81.59992747560547, -76.6142661520567, 41.34181133252104, -12.469328879159221)
COS = (0.9999992080920543, -19.73897953618229, 64.92862553583919, -85.27120644254374, 58.78833787867872, -21.067254412050286)
f32, bf16, i32 = jnp.float32, jnp.bfloat16, jnp.int32
VMEM_SPEC = pl.BlockSpec(memory_space=pltpu.VMEM)


def legendre_kernel(truncation, waves, spec_ref, leg_ref, out_ref, coeffs):
    slot = pl.program_id(0)
    rows = truncation + 2
    fields = spec_ref.shape[1]

    @pl.when(slot == 0)
    def _():
        coeffs[...] = jnp.zeros_like(coeffs)

    for field in range(fields):
        coeffs[2 * field : 2 * field + 2, 0:rows] = spec_ref[0, field]
    split = truncation + 1 - waves[slot]
    row = lax.broadcasted_iota(i32, (1, rows), 1)
    low = row < split
    offset = jnp.where(low, row, row - split)
    sign = jnp.where(offset % 2 == 0, 1.0, -1.0).astype(f32)
    low = jnp.where(low, 1.0, 0.0).astype(f32)
    high = 1.0 - low
    values = coeffs[:, 0:rows]
    stacked = jnp.concatenate([values * mask for mask in (low, low * sign, high, high * sign)], axis=0)
    stacked = stacked.astype(bf16)
    main = rows - 1
    sums = jnp.dot(stacked[:, 0:main], leg_ref[0, 0:main, :], preferred_element_type=f32)
    last = stacked[:, main:rows].astype(f32) * leg_ref[0, main:rows, :].astype(f32)
    sums = sums + last
    for half in range(2):
        for side in range(2):
            at = (2 * half + side) * ROWS
            out_ref[half, :, 128 * side : 128 * side + 128] = sums[at : at + ROWS, :]


def legendre_sums(wave_pairs, spectral, legendre):
    slots, rows, northern = legendre.shape
    fields = spectral.shape[3]
    parts = pltpu.with_memory_space_constraint(jnp.transpose(spectral, (0, 3, 2, 1)), pltpu.HBM)
    legendre = pltpu.with_memory_space_constraint(legendre, pltpu.HBM)
    return pl.pallas_call(
        functools.partial(legendre_kernel, rows - 2),
        out_shape=pltpu.VMEM((2 * slots, ROWS, 2 * northern), f32),
        grid_spec=pltpu.PrefetchScalarGridSpec(
            num_scalar_prefetch=1,
            grid=(slots,),
            in_specs=[
                pl.BlockSpec((1, fields, 2, rows), lambda p, w: (p, 0, 0, 0)),
                pl.BlockSpec((1, rows, northern), lambda p, w: (p, 0, 0)),
            ],
            out_specs=pl.BlockSpec((2, ROWS, 2 * northern), lambda p, w: (p, 0, 0)),
            scratch_shapes=[pltpu.VMEM((ROWS, 1408), f32)],
        ),
        compiler_params=pltpu.CompilerParams(vmem_limit_bytes=8 << 20),
    )(wave_pairs, parts, legendre)


def order_kernel(index_ref, sums_ref, out_ref, scratch):
    devices, lats = index_ref.shape[0], sums_ref.shape[2]
    index = index_ref[:, 0, :]
    lane = lax.broadcasted_iota(i32, (devices, lats), 1).astype(f32)
    onehot = jnp.concatenate(
        [jnp.where(index[:, 10 + j : 11 + j] == lane, 1.0, 0.0) for j in range(4)], axis=0
    ).astype(bf16)
    for t in range(TILES):
        part = sums_ref[GROUPS * t : GROUPS * (t + 1)].reshape(GROUPS * ROWS, lats)
        part = jnp.concatenate([part, jnp.zeros((128 - GROUPS * ROWS, lats), f32)], axis=0).astype(bf16)
        picked = lax.dot_general(onehot, part, (((1,), (1,)), ((), ())), preferred_element_type=f32)
        for j in range(4):
            scratch[pl.ds(j * TILES + t, devices, 4 * TILES), :] = picked[devices * j : devices * (j + 1), :]
    out_ref[...] = scratch[...].reshape(out_ref.shape).astype(bf16)


def order_latitudes(index, sums):
    devices = index.shape[0]
    return pl.pallas_call(
        order_kernel,
        out_shape=jax.ShapeDtypeStruct((devices, 4 * TILES, 128), bf16),
        in_specs=[VMEM_SPEC] * 2,
        out_specs=VMEM_SPEC,
        scratch_shapes=[pltpu.VMEM((devices * 4 * TILES, 128), f32)],
        compiler_params=pltpu.CompilerParams(vmem_limit_bytes=8 << 20),
    )(index, sums)


def poly(coefficients, y):
    total = jnp.full_like(y, coefficients[-1])
    for c in coefficients[-2::-1]:
        total = total * y + c
    return total


def sincos(product, n, inverse):
    turns = jnp.floor(product * inverse + 0.5)
    f = (product - turns * n) * inverse
    y = f * f
    return poly(COS, y), poly(SIN, y) * f


BLOCK = 128


def table_kernel(truncation, lat_rows, npoints, index_ref, out_ref, waves):
    l = pl.program_id(0)
    devices = index_ref.shape[0]
    depth = GROUPS * TILES * devices

    @pl.when(l == 0)
    def _():
        index = index_ref[:, 0, :]
        for g in range(GROUPS):
            for t in range(TILES):
                ph = GROUPS * t + g
                column = index[:, ph // 2 : ph // 2 + 1]
                if ph % 2:
                    column = truncation - column
                at = devices * (TILES * g + t)
                waves[at : at + devices, :] = jnp.broadcast_to(column, (devices, 128))

    odd = (2 * lax.broadcasted_iota(i32, (BLOCK, 128), 1) + 1).astype(f32)
    n = jnp.full((8, 128), 2 * npoints[lat_rows[l]], i32).astype(f32)
    inverse = (1.0 / n)[0:1]
    n = n[0:1]

    def rows_block(r, carry):
        at = pl.multiple_of(r * BLOCK, BLOCK)
        cosine, sine = sincos(waves[pl.ds(at, BLOCK), :] * odd, n, inverse)
        out_ref[0, pl.ds(at, BLOCK), :] = cosine.astype(bf16)
        out_ref[0, pl.ds(depth + at, BLOCK), :] = sine.astype(bf16)
        return carry

    lax.fori_loop(0, depth // BLOCK, rows_block, 0)


def fourier_tables(lat_rows, npoints, index, truncation):
    devices = index.shape[0]
    depth = GROUPS * TILES * devices
    return pl.pallas_call(
        functools.partial(table_kernel, float(truncation)),
        out_shape=pltpu.VMEM((4, 2 * depth, CHUNK // 2), bf16),
        grid_spec=pltpu.PrefetchScalarGridSpec(
            num_scalar_prefetch=2,
            grid=(4,),
            in_specs=[VMEM_SPEC],
            out_specs=pl.BlockSpec((1, 2 * depth, CHUNK // 2), lambda l, a, b: (l, 0, 0)),
            scratch_shapes=[pltpu.VMEM((depth, 128), f32)],
        ),
        compiler_params=pltpu.CompilerParams(vmem_limit_bytes=8 << 20),
    )(lat_rows, npoints, index)


BATCH = 8
LAST = ROW_PAIR // CHUNK
WIDTH = 128
DENSE = 208
REST = QUARTER - 10 * WIDTH


def synthesis_kernel(
    truncation, lat_rows, npoints, got_ref, wave_ref, select_ref, reverse_ref, table_ref, out_ref, got, parts, left, line, dense
):
    devices = got_ref.shape[0]
    rows = TILES * devices
    depth = GROUPS * rows
    lane = lax.broadcasted_iota(i32, (ROWS, WIDTH), 1)
    got[...] = got_ref[...].reshape(devices * 4 * TILES, WIDTH).astype(f32)
    for l in range(4):
        stacked = jnp.concatenate(
            [got[pl.ds(l * TILES + t, devices, 4 * TILES), :] for t in range(TILES)], axis=0
        ).astype(bf16)
        both = lax.dot_general(select_ref[...], stacked, (((1,), (1,)), ((), ())), preferred_element_type=f32)
        for g in range(GROUPS):
            k = wave_ref[:, g * rows : (g + 1) * rows]
            row = lax.broadcasted_iota(i32, (ROWS, rows), 0)
            scale = jnp.where(row < 10, 1.0, jnp.broadcast_to(k / truncation, (ROWS, rows)))
            at = 2 * ROWS * g
            for c in range(2):
                part = both[at + c * ROWS : at + (c + 1) * ROWS] * scale
                parts[l, c, :, g * rows : (g + 1) * rows] = part.astype(bf16).astype(f32)

    def batch(l, first, origin):
        n = jnp.full((8, WIDTH), 2 * npoints[lat_rows[l]], i32).astype(f32)
        inverse = (1.0 / n)[0:1, 0:1]
        n = n[0:1, 0:1]
        chunk = lax.broadcasted_iota(i32, (BATCH, rows), 0)
        center = (2 * CHUNK * (first + chunk) - 2 * origin + CHUNK - 1).astype(f32)
        for g in range(GROUPS):
            at = slice(g * rows, (g + 1) * rows)
            at_imag = slice(depth + g * rows, depth + (g + 1) * rows)
            k = wave_ref[:, at]
            weight = jnp.where(4.0 * k < n, jnp.where(k == 0.0, 1.0, 2.0), 0.0)
            cosine, sine = sincos(center * k, n, inverse)
            cosine, sine = cosine * weight, sine * weight
            real, imag = parts[l, 0, :, at], parts[l, 1, :, at]
            for j in range(0, BATCH, 2):
                turned = [
                    (real * cosine[i : i + 1] - imag * sine[i : i + 1], imag * cosine[i : i + 1] + real * sine[i : i + 1])
                    for i in (j, j + 1)
                ]
                to = slice(j * ROWS, (j + 2) * ROWS)
                left[to, at] = jnp.concatenate([turned[0][0], turned[1][0]], axis=0).astype(bf16)
                left[to, at_imag] = jnp.concatenate([turned[0][1], turned[1][1]], axis=0).astype(bf16)
        even = jnp.dot(left[:, 0:depth], table_ref[l, 0:depth], preferred_element_type=f32)
        odd = jnp.dot(left[:, depth : 2 * depth], table_ref[l, depth : 2 * depth], preferred_element_type=f32)
        before, after = even + odd, even - odd
        for j in range(BATCH):
            tile = 2 * (first + j)
            at = slice(j * ROWS, (j + 1) * ROWS)
            line[tile] = jnp.where(WIDTH - 1 - lane + tile * WIDTH >= origin, before[at], line[tile])
            line[tile + 1] = jnp.where(lane + (tile + 1) * WIDTH >= origin, after[at], line[tile + 1])

    for pair in range(2):
        n_a = npoints[lat_rows[2 * pair]]
        start_b = lax.shift_right_arithmetic(n_a, 8)
        batches_a = lax.shift_right_arithmetic(lax.shift_right_arithmetic(n_a - 1, 8) + BATCH, 3)
        batches_b = lax.shift_right_arithmetic(LAST - start_b + BATCH, 3)

        def body(step, carry):
            second = step >= batches_a
            l = 2 * pair + jnp.where(second, 1, 0)
            first = jnp.where(second, start_b + BATCH * (step - batches_a), BATCH * step)
            batch(l, first, jnp.where(second, n_a, 0))
            return carry

        lax.fori_loop(0, batches_a + batches_b, body, 0)
        before = jnp.concatenate([line[2 * i] for i in range(LAST + 1)], axis=0).astype(bf16)
        before = jnp.dot(before, reverse_ref[...], preferred_element_type=f32)
        for i in range(LAST + 1):
            line[2 * i] = before[i * ROWS : (i + 1) * ROWS]
        for q in range(4):
            shift = (QUARTER * q) % WIDTH
            for i in range(QUARTER // WIDTH + 1):
                tile = QUARTER * q // WIDTH + i
                v = line[tile]
                if shift:
                    v = jnp.where(
                        lane < WIDTH - shift,
                        pltpu.roll(v, WIDTH - shift, 1),
                        pltpu.roll(line[tile + 1], WIDTH - shift, 1),
                    )
                if i < 10:
                    dense[q, 20 * i : 20 * i + 20] = v[0:20]
                else:
                    spread = lane[0:8]
                    dense[q, 200:208] = jnp.where(
                        spread < 16, v[0:8], jnp.where(spread < 32, pltpu.roll(v[8:16], 16, 1), pltpu.roll(v[16:24], 32, 1))
                    )
            out_ref[4 * pair + q] = dense[q].astype(bf16)


def select_rows():
    table = np.zeros((GROUPS, 2 * ROWS, 128), np.float32)
    for g in range(GROUPS):
        for f in range(10):
            real, imag = g * ROWS + 2 * f, g * ROWS + 2 * f + 1
            table[g, f, real] = 1.0
            table[g, 10 + f, imag] = -1.0
            table[g, ROWS + f, imag] = 1.0
            table[g, ROWS + 10 + f, real] = 1.0
    return table.reshape(GROUPS * 2 * ROWS, 128).astype(jnp.bfloat16)


def synthesis(lat_rows, npoints, received, wave_line, tables, truncation):
    devices = received.shape[0]
    depth = GROUPS * TILES * devices
    reverse = np.eye(WIDTH)[::-1].astype(jnp.bfloat16)
    return pl.pallas_call(
        functools.partial(synthesis_kernel, float(truncation)),
        out_shape=jax.ShapeDtypeStruct((8, DENSE, WIDTH), bf16),
        in_specs=[pl.BlockSpec(memory_space=pltpu.SMEM)] * 2 + [VMEM_SPEC] * 5,
        out_specs=VMEM_SPEC,
        scratch_shapes=[
            pltpu.VMEM((devices * 4 * TILES, WIDTH), f32),
            pltpu.VMEM((4, 2, ROWS, depth), f32),
            pltpu.VMEM((BATCH * ROWS, 2 * depth), bf16),
            pltpu.VMEM((2 * (LAST + BATCH) + 2, ROWS, WIDTH), f32),
            pltpu.VMEM((4, DENSE, WIDTH), f32),
        ],
        compiler_params=pltpu.CompilerParams(vmem_limit_bytes=16 << 20),
    )(lat_rows, npoints, received, wave_line, select_rows(), reverse, tables)


def place_kernel(in_ref, out_ref, dense, placed):
    for source in range(in_ref.shape[0]):
        dense[source] = in_ref[source].astype(f32)
        rest = dense[source, 200:208]
        rest = jnp.concatenate([rest, pltpu.roll(rest, WIDTH - 16, 1), pltpu.roll(rest, WIDTH - 32, 1)], axis=0)
        for kind in range(2):
            to = slice(10 * source, 10 * source + 10)
            for i in range(10):
                at = 20 * i + 10 * kind
                placed[kind, to, WIDTH * i : WIDTH * i + WIDTH] = dense[source, at : at + 10]
            placed[kind, to, 10 * WIDTH : QUARTER] = rest[10 * kind : 10 * kind + 10, 0:REST]
    out_ref[...] = placed[:, :, 0:QUARTER].astype(bf16)


def place(blocks):
    sources = blocks.shape[0]
    return pl.pallas_call(
        place_kernel,
        out_shape=jax.ShapeDtypeStruct((2, 10 * sources, QUARTER), bf16),
        in_specs=[VMEM_SPEC],
        out_specs=VMEM_SPEC,
        scratch_shapes=[
            pltpu.VMEM((sources, DENSE, WIDTH), f32),
            pltpu.VMEM((2, 10 * sources, 11 * WIDTH), f32),
        ],
        compiler_params=pltpu.CompilerParams(vmem_limit_bytes=8 << 20),
    )(blocks)


def wave_line_of(index, truncation):
    low = jnp.transpose(index[:, 0, 0:10])
    both = jnp.stack([low, truncation - low], axis=1)
    both = both.reshape(TILES, GROUPS, index.shape[0])
    return jnp.transpose(both, (1, 0, 2)).reshape(1, -1)


def on_device(spectral, legendre, wave_pairs, npoints, lat_rows):
    truncation = legendre.shape[1] - 2
    devices = lax.axis_size("wave")
    mine = jnp.concatenate([wave_pairs, lat_rows]).astype(f32)
    mine = jnp.pad(mine, (0, 128 - mine.shape[0]))
    index = lax.all_to_all(jnp.broadcast_to(mine[None, None, :], (devices, 1, 128)), "wave", 0, 0, tiled=True)
    sums = legendre_sums(wave_pairs, spectral, legendre)
    ordered = order_latitudes(index, sums)
    received = lax.all_to_all(ordered, "wave", 0, 0, tiled=True)
    tables = fourier_tables(lat_rows, npoints, index, truncation)
    wave_line = wave_line_of(index, float(truncation))
    blocks = synthesis(lat_rows, npoints, received, wave_line, tables, truncation)
    blocks = lax.all_to_all(blocks, "field", 0, 0, tiled=True)
    return place(blocks)


def solution(mesh):
    placed = (P("wave", None, None, "field"), P("wave", None, None), P("wave"), P(), P("wave"))
    return jax.shard_map(
        on_device,
        mesh=mesh,
        in_specs=placed,
        out_specs=P(None, None, ("wave", "field")),
        check_vma=False,
    )
```

```python
import functools

import jax
import jax.numpy as jnp
import numpy as np
from jax import lax
from jax.experimental import pallas as pl
from jax.experimental.pallas import tpu as pltpu
from jax.sharding import PartitionSpec as P

ROW_PAIR = 5156
QUARTER = ROW_PAIR // 4
CHUNK = 256
GROUPS = 5
TILES = 4
ROWS = 24
SIN = (6.283184915155849, -41.3415888250942, 81.59992747560547, -76.6142661520567, 41.34181133252104, -12.469328879159221)
COS = (0.9999992080920543, -19.73897953618229, 64.92862553583919, -85.27120644254374, 58.78833787867872, -21.067254412050286)
f32, bf16, i32 = jnp.float32, jnp.bfloat16, jnp.int32
VMEM_SPEC = pl.BlockSpec(memory_space=pltpu.VMEM)


def legendre_kernel(truncation, waves, spec_ref, leg_ref, out_ref, coeffs):
    slot = pl.program_id(0)
    rows = truncation + 2
    fields = spec_ref.shape[1]

    @pl.when(slot == 0)
    def _():
        coeffs[...] = jnp.zeros_like(coeffs)

    for field in range(fields):
        coeffs[2 * field : 2 * field + 2, 0:rows] = spec_ref[0, field]
    split = truncation + 1 - waves[slot]
    row = lax.broadcasted_iota(i32, (1, rows), 1)
    low = row < split
    offset = jnp.where(low, row, row - split)
    sign = jnp.where(offset % 2 == 0, 1.0, -1.0).astype(f32)
    low = jnp.where(low, 1.0, 0.0).astype(f32)
    high = 1.0 - low
    values = coeffs[:, 0:rows]
    stacked = jnp.concatenate([values * mask for mask in (low, low * sign, high, high * sign)], axis=0)
    stacked = stacked.astype(bf16)
    main = rows - 1
    sums = jnp.dot(stacked[:, 0:main], leg_ref[0, 0:main, :], preferred_element_type=f32)
    last = stacked[:, main:rows].astype(f32) * leg_ref[0, main:rows, :].astype(f32)
    sums = sums + last
    for half in range(2):
        for side in range(2):
            at = (2 * half + side) * ROWS
            out_ref[half, :, 128 * side : 128 * side + 128] = sums[at : at + ROWS, :]


def legendre_sums(wave_pairs, spectral, legendre):
    slots, rows, northern = legendre.shape
    fields = spectral.shape[3]
    parts = pltpu.with_memory_space_constraint(jnp.transpose(spectral, (0, 3, 2, 1)), pltpu.HBM)
    legendre = pltpu.with_memory_space_constraint(legendre, pltpu.HBM)
    return pl.pallas_call(
        functools.partial(legendre_kernel, rows - 2),
        out_shape=pltpu.VMEM((2 * slots, ROWS, 2 * northern), f32),
        grid_spec=pltpu.PrefetchScalarGridSpec(
            num_scalar_prefetch=1,
            grid=(slots,),
            in_specs=[
                pl.BlockSpec((1, fields, 2, rows), lambda p, w: (p, 0, 0, 0)),
                pl.BlockSpec((1, rows, northern), lambda p, w: (p, 0, 0)),
            ],
            out_specs=pl.BlockSpec((2, ROWS, 2 * northern), lambda p, w: (p, 0, 0)),
            scratch_shapes=[pltpu.VMEM((ROWS, 1408), f32)],
        ),
        compiler_params=pltpu.CompilerParams(vmem_limit_bytes=8 << 20),
    )(wave_pairs, parts, legendre)


def order_kernel(index_ref, sums_ref, out_ref, scratch):
    devices, lats = index_ref.shape[0], sums_ref.shape[2]
    index = index_ref[:, 0, :]
    lane = lax.broadcasted_iota(i32, (devices, lats), 1).astype(f32)
    onehot = jnp.concatenate(
        [jnp.where(index[:, 10 + j : 11 + j] == lane, 1.0, 0.0) for j in range(4)], axis=0
    ).astype(bf16)
    for t in range(TILES):
        part = sums_ref[GROUPS * t : GROUPS * (t + 1)].reshape(GROUPS * ROWS, lats)
        part = jnp.concatenate([part, jnp.zeros((128 - GROUPS * ROWS, lats), f32)], axis=0).astype(bf16)
        picked = lax.dot_general(onehot, part, (((1,), (1,)), ((), ())), preferred_element_type=f32)
        for j in range(4):
            scratch[pl.ds(j * TILES + t, devices, 4 * TILES), :] = picked[devices * j : devices * (j + 1), :]
    out_ref[...] = scratch[...].reshape(out_ref.shape).astype(bf16)


def order_latitudes(index, sums):
    devices = index.shape[0]
    return pl.pallas_call(
        order_kernel,
        out_shape=jax.ShapeDtypeStruct((devices, 4 * TILES, 128), bf16),
        in_specs=[VMEM_SPEC] * 2,
        out_specs=VMEM_SPEC,
        scratch_shapes=[pltpu.VMEM((devices * 4 * TILES, 128), f32)],
        compiler_params=pltpu.CompilerParams(vmem_limit_bytes=8 << 20),
    )(index, sums)


def poly(coefficients, y):
    total = jnp.full_like(y, coefficients[-1])
    for c in coefficients[-2::-1]:
        total = total * y + c
    return total


def sincos(product, n, inverse):
    turns = jnp.floor(product * inverse + 0.5)
    f = (product - turns * n) * inverse
    y = f * f
    return poly(COS, y), poly(SIN, y) * f


BLOCK = 128


def table_kernel(truncation, lat_rows, npoints, index_ref, out_ref, waves):
    l = pl.program_id(0)
    devices = index_ref.shape[0]
    depth = GROUPS * TILES * devices

    @pl.when(l == 0)
    def _():
        index = index_ref[:, 0, :]
        for g in range(GROUPS):
            for t in range(TILES):
                ph = GROUPS * t + g
                column = index[:, ph // 2 : ph // 2 + 1]
                if ph % 2:
                    column = truncation - column
                at = devices * (TILES * g + t)
                waves[at : at + devices, :] = jnp.broadcast_to(column, (devices, 128))

    odd = (2 * lax.broadcasted_iota(i32, (BLOCK, 128), 1) + 1).astype(f32)
    n = jnp.full((8, 128), 2 * npoints[lat_rows[l]], i32).astype(f32)
    inverse = (1.0 / n)[0:1]
    n = n[0:1]

    def rows_block(r, carry):
        at = pl.multiple_of(r * BLOCK, BLOCK)
        cosine, sine = sincos(waves[pl.ds(at, BLOCK), :] * odd, n, inverse)
        out_ref[0, pl.ds(at, BLOCK), :] = cosine.astype(bf16)
        out_ref[0, pl.ds(depth + at, BLOCK), :] = sine.astype(bf16)
        return carry

    lax.fori_loop(0, depth // BLOCK, rows_block, 0)


def fourier_tables(lat_rows, npoints, index, truncation):
    devices = index.shape[0]
    depth = GROUPS * TILES * devices
    return pl.pallas_call(
        functools.partial(table_kernel, float(truncation)),
        out_shape=pltpu.VMEM((4, 2 * depth, CHUNK // 2), bf16),
        grid_spec=pltpu.PrefetchScalarGridSpec(
            num_scalar_prefetch=2,
            grid=(4,),
            in_specs=[VMEM_SPEC],
            out_specs=pl.BlockSpec((1, 2 * depth, CHUNK // 2), lambda l, a, b: (l, 0, 0)),
            scratch_shapes=[pltpu.VMEM((depth, 128), f32)],
        ),
        compiler_params=pltpu.CompilerParams(vmem_limit_bytes=8 << 20),
    )(lat_rows, npoints, index)


BATCH = 8
BATCHES = 3
WIDTH = 128
FIELDS = 10
DENSE = 104
REST = QUARTER - 10 * WIDTH
PART = 16


def synthesis_kernel(
    truncation, kind, lat_rows, npoints, got_ref, wave_ref, select_ref, reverse_ref, table_ref, out_ref, got, parts, left, line, dense
):
    devices = got_ref.shape[0]
    rows = TILES * devices
    depth = GROUPS * rows
    chunks = BATCH * BATCHES
    got[...] = got_ref[...].reshape(devices * 4 * TILES, WIDTH).astype(f32)
    for l in range(4):
        stacked = jnp.concatenate(
            [got[pl.ds(l * TILES + t, devices, 4 * TILES), :] for t in range(TILES)], axis=0
        ).astype(bf16)
        both = lax.dot_general(select_ref[...], stacked, (((1,), (1,)), ((), ())), preferred_element_type=f32)
        for g in range(GROUPS):
            for c in range(2):
                at = PART * (2 * g + c)
                part = both[at : at + PART]
                if kind:
                    part = part * (wave_ref[:, g * rows : (g + 1) * rows] / truncation)
                    part = part.astype(bf16).astype(f32)
                parts[l, c, :, g * rows : (g + 1) * rows] = part

    chunk = lax.broadcasted_iota(i32, (BATCH, rows), 0)
    place_in = lax.broadcasted_iota(i32, (BATCH, WIDTH), 0) * CHUNK + lax.broadcasted_iota(i32, (BATCH, WIDTH), 1)
    place_back = lax.broadcasted_iota(i32, (BATCH, WIDTH), 0) * CHUNK - lax.broadcasted_iota(i32, (BATCH, WIDTH), 1)

    def batch(l, first, origin):
        n = jnp.full((8, WIDTH), 2 * npoints[lat_rows[l]], i32).astype(f32)
        inverse = (1.0 / n)[0:1, 0:1]
        n = n[0:1, 0:1]
        center = (2 * CHUNK * (first + chunk) - 2 * origin + CHUNK - 1).astype(f32)
        for g in range(GROUPS):
            at = slice(g * rows, (g + 1) * rows)
            at_imag = slice(depth + g * rows, depth + (g + 1) * rows)
            k = wave_ref[:, at]
            weight = jnp.where(4.0 * k < n, jnp.where(k == 0.0, 1.0, 2.0), 0.0)
            cosine, sine = sincos(center * k, n, inverse)
            cosine, sine = cosine * weight, sine * weight
            for f in range(0, FIELDS, 2):
                turned_real, turned_imag = [], []
                for i in (f, f + 1):
                    real, imag = parts[l, 0, i : i + 1, at], parts[l, 1, i : i + 1, at]
                    turned_real.append(real * cosine - imag * sine)
                    turned_imag.append(imag * cosine + real * sine)
                to = slice(f * BATCH, (f + 2) * BATCH)
                left[to, at] = jnp.concatenate(turned_real, axis=0).astype(bf16)
                left[to, at_imag] = jnp.concatenate(turned_imag, axis=0).astype(bf16)
        even = jnp.dot(left[:, 0:depth], table_ref[l, 0:depth], preferred_element_type=f32)
        odd = jnp.dot(left[:, depth : 2 * depth], table_ref[l, depth : 2 * depth], preferred_element_type=f32)
        before, after = even + odd, even - odd
        limit = origin - CHUNK * first
        keep_back = place_back + (WIDTH - 1) >= limit
        keep_in = place_in + WIDTH >= limit
        for f in range(FIELDS):
            at = slice(f * BATCH, (f + 1) * BATCH)
            to = pl.ds(pl.multiple_of(f * chunks + first, 8), BATCH)
            line[to] = jnp.where(keep_back, before[at], line[to])
            to = pl.ds(pl.multiple_of((FIELDS + f) * chunks + first, 8), BATCH)
            line[to] = jnp.where(keep_in, after[at], line[to])

    lane = lax.broadcasted_iota(i32, (FIELDS, WIDTH), 1)
    for pair in range(2):
        n_a = npoints[lat_rows[2 * pair]]
        batches_a = lax.shift_right_arithmetic(n_a - 1, 11) + 1
        start_b = lax.shift_right_arithmetic(n_a, 11)

        def body(step, carry):
            second = step >= batches_a
            l = 2 * pair + jnp.where(second, 1, 0)
            first = BATCH * jnp.where(second, step - batches_a + start_b, step)
            batch(l, first, jnp.where(second, n_a, 0))
            return carry

        lax.fori_loop(0, batches_a + BATCHES - start_b, body, 0)
        back = slice(0, FIELDS * chunks)
        line[back] = jnp.dot(line[back].astype(bf16), reverse_ref[...], preferred_element_type=f32)

        def tile_of(tile):
            return line[pl.ds((tile % 2) * FIELDS * chunks + tile // 2, FIELDS, chunks), :]

        for q in range(4):
            shift = (QUARTER * q) % WIDTH
            for i in range(QUARTER // WIDTH + 1):
                tile = QUARTER * q // WIDTH + i
                v = tile_of(tile)
                if shift:
                    v = jnp.where(
                        lane < WIDTH - shift,
                        pltpu.roll(v, WIDTH - shift, 1),
                        pltpu.roll(tile_of(tile + 1), WIDTH - shift, 1),
                    )
                if i < 10:
                    dense[q, FIELDS * i : FIELDS * i + FIELDS] = v
                else:
                    dense[q, 100:104] = v[0:4]
                    dense[q, 100:104, 16:32] = v[4:8, 0:16]
                    dense[q, 100:102, 32:48] = v[8:10, 0:16]
            out_ref[4 * pair + q] = dense[q].astype(bf16)


def select_rows(kind):
    table = np.zeros((GROUPS, 2, PART, 128), np.float32)
    for g in range(GROUPS):
        for f in range(FIELDS):
            real, imag = g * ROWS + 2 * f, g * ROWS + 2 * f + 1
            if kind == 0:
                table[g, 0, f, real] = 1.0
                table[g, 1, f, imag] = 1.0
            else:
                table[g, 0, f, imag] = -1.0
                table[g, 1, f, real] = 1.0
    return table.reshape(GROUPS * 2 * PART, 128).astype(jnp.bfloat16)


def synthesis(kind, lat_rows, npoints, received, wave_line, tables, truncation):
    devices = received.shape[0]
    depth = GROUPS * TILES * devices
    reverse = np.eye(WIDTH)[::-1].astype(jnp.bfloat16)
    return pl.pallas_call(
        functools.partial(synthesis_kernel, float(truncation), kind),
        out_shape=jax.ShapeDtypeStruct((8, DENSE, WIDTH), bf16),
        in_specs=[pl.BlockSpec(memory_space=pltpu.SMEM)] * 2 + [VMEM_SPEC] * 5,
        out_specs=VMEM_SPEC,
        scratch_shapes=[
            pltpu.VMEM((devices * 4 * TILES, WIDTH), f32),
            pltpu.VMEM((4, 2, PART, depth), f32),
            pltpu.VMEM((BATCH * FIELDS, 2 * depth), bf16),
            pltpu.VMEM((2 * FIELDS * BATCH * BATCHES, WIDTH), f32),
            pltpu.VMEM((4, DENSE, WIDTH), f32),
        ],
        compiler_params=pltpu.CompilerParams(vmem_limit_bytes=16 << 20),
    )(lat_rows, npoints, received, wave_line, select_rows(kind), reverse, tables)


def place_kernel(value_ref, slope_ref, out_ref, dense, placed):
    for source in range(value_ref.shape[0]):
        for kind, in_ref in enumerate((value_ref, slope_ref)):
            dense[source] = in_ref[source].astype(f32)
            to = slice(FIELDS * source, FIELDS * source + FIELDS)
            for i in range(10):
                placed[kind, to, WIDTH * i : WIDTH * i + WIDTH] = dense[source, FIELDS * i : FIELDS * i + FIELDS]
            rest = dense[source, 100:104]
            rest = jnp.concatenate([rest[:, 0:16], rest[:, 16:32], rest[0:2, 32:48]], axis=0)
            placed[kind, to, 10 * WIDTH : QUARTER] = rest[:, 0:REST]
    out_ref[...] = placed[:, :, 0:QUARTER].astype(bf16)


def place(values, slopes):
    sources = values.shape[0]
    return pl.pallas_call(
        place_kernel,
        out_shape=jax.ShapeDtypeStruct((2, FIELDS * sources, QUARTER), bf16),
        in_specs=[VMEM_SPEC] * 2,
        out_specs=VMEM_SPEC,
        scratch_shapes=[
            pltpu.VMEM((sources, DENSE, WIDTH), f32),
            pltpu.VMEM((2, FIELDS * sources, 11 * WIDTH), f32),
        ],
        compiler_params=pltpu.CompilerParams(vmem_limit_bytes=8 << 20),
    )(values, slopes)


def wave_line_of(index, truncation):
    low = jnp.transpose(index[:, 0, 0:10])
    both = jnp.stack([low, truncation - low], axis=1)
    both = both.reshape(TILES, GROUPS, index.shape[0])
    return jnp.transpose(both, (1, 0, 2)).reshape(1, -1)


def on_device(spectral, legendre, wave_pairs, npoints, lat_rows):
    truncation = legendre.shape[1] - 2
    devices = lax.axis_size("wave")
    mine = jnp.concatenate([wave_pairs, lat_rows]).astype(f32)
    mine = jnp.pad(mine, (0, 128 - mine.shape[0]))
    index = lax.all_to_all(jnp.broadcast_to(mine[None, None, :], (devices, 1, 128)), "wave", 0, 0, tiled=True)
    sums = legendre_sums(wave_pairs, spectral, legendre)
    ordered = order_latitudes(index, sums)
    received = lax.all_to_all(ordered, "wave", 0, 0, tiled=True)
    tables = fourier_tables(lat_rows, npoints, index, truncation)
    wave_line = wave_line_of(index, float(truncation))
    blocks = []
    for kind in range(2):
        block = synthesis(kind, lat_rows, npoints, received, wave_line, tables, truncation)
        blocks.append(lax.all_to_all(block, "field", 0, 0, tiled=True))
    return place(*blocks)


def solution(mesh):
    placed = (P("wave", None, None, "field"), P("wave", None, None), P("wave"), P(), P("wave"))
    return jax.shard_map(
        on_device,
        mesh=mesh,
        in_specs=placed,
        out_specs=P(None, None, ("wave", "field")),
        check_vma=False,
    )
```

```python
import functools

import jax
import jax.numpy as jnp
import numpy as np
from jax import lax
from jax.experimental import pallas as pl
from jax.experimental.pallas import tpu as pltpu
from jax.sharding import PartitionSpec as P

ROW_PAIR = 5156
QUARTER = ROW_PAIR // 4
CHUNK = 256
GROUPS = 5
TILES = 4
ROWS = 24
SIN = (6.283184915155849, -41.3415888250942, 81.59992747560547, -76.6142661520567, 41.34181133252104, -12.469328879159221)
COS = (0.9999992080920543, -19.73897953618229, 64.92862553583919, -85.27120644254374, 58.78833787867872, -21.067254412050286)
f32, bf16, i32 = jnp.float32, jnp.bfloat16, jnp.int32
VMEM_SPEC = pl.BlockSpec(memory_space=pltpu.VMEM)


def legendre_kernel(truncation, waves, spec_hbm, leg_hbm, out_ref, spec_ref, leg_ref, coeffs, spec_sems, leg_sems):
    rows = truncation + 2
    slots, fields = spec_ref.shape[0], spec_ref.shape[1]
    main = rows - 1

    def copies(slot):
        return (
            pltpu.make_async_copy(spec_hbm.at[slot], spec_ref.at[slot], spec_sems.at[slot]),
            pltpu.make_async_copy(leg_hbm.at[slot], leg_ref.at[slot], leg_sems.at[slot]),
        )

    for slot in range(slots):
        for copy in copies(slot):
            copy.start()
    coeffs[...] = jnp.zeros_like(coeffs)

    def body(slot, carry):
        for copy in copies(slot):
            copy.wait()
        for field in range(fields):
            coeffs[2 * field : 2 * field + 2, 0:rows] = spec_ref[slot, field]
        split = truncation + 1 - waves[slot]
        row = lax.broadcasted_iota(i32, (1, rows), 1)
        low = row < split
        offset = jnp.where(low, row, row - split)
        sign = jnp.where(offset % 2 == 0, 1.0, -1.0).astype(f32)
        low = jnp.where(low, 1.0, 0.0).astype(f32)
        high = 1.0 - low
        values = coeffs[:, 0:rows]
        stacked = jnp.concatenate([values * mask for mask in (low, low * sign, high, high * sign)], axis=0)
        stacked = stacked.astype(bf16)
        sums = jnp.dot(stacked[:, 0:main], leg_ref[slot, 0:main, :], preferred_element_type=f32)
        last = stacked[:, main:rows].astype(f32) * leg_ref[slot, main:rows, :].astype(f32)
        sums = sums + last
        for half in range(2):
            for side in range(2):
                at = (2 * half + side) * ROWS
                out_ref[2 * slot + half, :, 128 * side : 128 * side + 128] = sums[at : at + ROWS, :]
        return carry

    lax.fori_loop(0, slots, body, 0)


def legendre_sums(wave_pairs, spectral, legendre):
    slots, rows, northern = legendre.shape
    fields = spectral.shape[3]
    parts = pltpu.with_memory_space_constraint(jnp.transpose(spectral, (0, 3, 2, 1)), pltpu.HBM)
    legendre = pltpu.with_memory_space_constraint(legendre, pltpu.HBM)
    return pl.pallas_call(
        functools.partial(legendre_kernel, rows - 2),
        out_shape=pltpu.VMEM((2 * slots, ROWS, 2 * northern), f32),
        in_specs=[pl.BlockSpec(memory_space=pltpu.SMEM)] + [pl.BlockSpec(memory_space=pltpu.HBM)] * 2,
        out_specs=VMEM_SPEC,
        scratch_shapes=[
            pltpu.VMEM((slots, fields, 2, rows), f32),
            pltpu.VMEM((slots, rows, northern), bf16),
            pltpu.VMEM((ROWS, 1408), f32),
            pltpu.SemaphoreType.DMA((slots,)),
            pltpu.SemaphoreType.DMA((slots,)),
        ],
        compiler_params=pltpu.CompilerParams(vmem_limit_bytes=16 << 20),
    )(pltpu.with_memory_space_constraint(wave_pairs, pltpu.HBM), parts, legendre)


def announce_kernel(waves, lats, out_ref):
    lane = lax.broadcasted_iota(i32, (1, 128), 1)
    row = jnp.zeros((1, 128), i32)
    for i in range(14):
        row = jnp.where(lane == i, waves[i] if i < 10 else lats[i - 10], row)
    out_ref[...] = jnp.broadcast_to(row.astype(f32).reshape(1, 1, 128), out_ref.shape)


def announcement(wave_pairs, lat_rows, devices):
    return pl.pallas_call(
        announce_kernel,
        out_shape=jax.ShapeDtypeStruct((devices, 1, 128), f32),
        in_specs=[pl.BlockSpec(memory_space=pltpu.SMEM)] * 2,
        out_specs=VMEM_SPEC,
        compiler_params=pltpu.CompilerParams(vmem_limit_bytes=1 << 20),
    )(*(pltpu.with_memory_space_constraint(x, pltpu.HBM) for x in (wave_pairs, lat_rows)))


def order_kernel(index_ref, sums_ref, out_ref, scratch):
    devices, lats = index_ref.shape[0], sums_ref.shape[2]
    index = index_ref[:, 0, :]
    lane = lax.broadcasted_iota(i32, (devices, lats), 1).astype(f32)
    onehot = jnp.concatenate(
        [jnp.where(index[:, 10 + j : 11 + j] == lane, 1.0, 0.0) for j in range(4)], axis=0
    ).astype(bf16)
    for t in range(TILES):
        part = sums_ref[GROUPS * t : GROUPS * (t + 1)].reshape(GROUPS * ROWS, lats)
        part = jnp.concatenate([part, jnp.zeros((128 - GROUPS * ROWS, lats), f32)], axis=0).astype(bf16)
        picked = lax.dot_general(onehot, part, (((1,), (1,)), ((), ())), preferred_element_type=f32)
        for j in range(4):
            scratch[pl.ds(j * TILES + t, devices, 4 * TILES), :] = picked[devices * j : devices * (j + 1), :]
    out_ref[...] = scratch[...].reshape(out_ref.shape).astype(bf16)


def order_latitudes(index, sums):
    devices = index.shape[0]
    return pl.pallas_call(
        order_kernel,
        out_shape=jax.ShapeDtypeStruct((devices, 4 * TILES, 128), bf16),
        in_specs=[VMEM_SPEC] * 2,
        out_specs=VMEM_SPEC,
        scratch_shapes=[pltpu.VMEM((devices * 4 * TILES, 128), f32)],
        compiler_params=pltpu.CompilerParams(vmem_limit_bytes=8 << 20),
    )(index, sums)


def poly(coefficients, y):
    total = jnp.full_like(y, coefficients[-1])
    for c in coefficients[-2::-1]:
        total = total * y + c
    return total


def sincos(product, n, inverse):
    turns = jnp.floor(product * inverse + 0.5)
    f = (product - turns * n) * inverse
    y = f * f
    return poly(COS, y), poly(SIN, y) * f


BLOCK = 128


def table_kernel(truncation, lat_rows, npoints, index_ref, out_ref, waves):
    l = pl.program_id(0)
    devices = index_ref.shape[0]
    depth = GROUPS * TILES * devices

    @pl.when(l == 0)
    def _():
        index = index_ref[:, 0, :]
        for g in range(GROUPS):
            for t in range(TILES):
                ph = GROUPS * t + g
                column = index[:, ph // 2 : ph // 2 + 1]
                if ph % 2:
                    column = truncation - column
                at = devices * (TILES * g + t)
                waves[at : at + devices, :] = jnp.broadcast_to(column, (devices, 128))

    odd = (2 * lax.broadcasted_iota(i32, (BLOCK, 128), 1) + 1).astype(f32)
    n = jnp.full((8, 128), 2 * npoints[lat_rows[l]], i32).astype(f32)
    inverse = (1.0 / n)[0:1]
    n = n[0:1]

    def rows_block(r, carry):
        at = pl.multiple_of(r * BLOCK, BLOCK)
        cosine, sine = sincos(waves[pl.ds(at, BLOCK), :] * odd, n, inverse)
        out_ref[0, pl.ds(at, BLOCK), :] = cosine.astype(bf16)
        out_ref[0, pl.ds(depth + at, BLOCK), :] = sine.astype(bf16)
        return carry

    lax.fori_loop(0, depth // BLOCK, rows_block, 0)


def fourier_tables(lat_rows, npoints, index, truncation):
    devices = index.shape[0]
    depth = GROUPS * TILES * devices
    return pl.pallas_call(
        functools.partial(table_kernel, float(truncation)),
        out_shape=pltpu.VMEM((4, 2 * depth, CHUNK // 2), bf16),
        grid_spec=pltpu.PrefetchScalarGridSpec(
            num_scalar_prefetch=2,
            grid=(4,),
            in_specs=[VMEM_SPEC],
            out_specs=pl.BlockSpec((1, 2 * depth, CHUNK // 2), lambda l, a, b: (l, 0, 0)),
            scratch_shapes=[pltpu.VMEM((depth, 128), f32)],
        ),
        compiler_params=pltpu.CompilerParams(vmem_limit_bytes=8 << 20),
    )(lat_rows, npoints, index)


BATCH = 8
BATCHES = 3
WIDTH = 128
COLUMNS = 20
DENSE = 208
REST = QUARTER - 10 * WIDTH


def synthesis_kernel(
    truncation, lat_rows, npoints, got_ref, wave_ref, select_ref, reverse_ref, table_ref, out_ref, got, parts, left, line, dense
):
    devices = got_ref.shape[0]
    rows = TILES * devices
    depth = GROUPS * rows
    chunks = BATCH * BATCHES
    got[...] = got_ref[...].reshape(devices * 4 * TILES, WIDTH).astype(f32)
    for l in range(4):
        stacked = jnp.concatenate(
            [got[pl.ds(l * TILES + t, devices, 4 * TILES), :] for t in range(TILES)], axis=0
        ).astype(bf16)
        both = lax.dot_general(select_ref[...], stacked, (((1,), (1,)), ((), ())), preferred_element_type=f32)
        for g in range(GROUPS):
            at = slice(g * rows, (g + 1) * rows)
            row = lax.broadcasted_iota(i32, (ROWS, rows), 0)
            scale = jnp.where(row < 10, 1.0, jnp.broadcast_to(wave_ref[:, at] / truncation, (ROWS, rows)))
            for c in range(2):
                part = both[ROWS * (2 * g + c) : ROWS * (2 * g + c + 1)] * scale
                parts[l, c, :, at] = part.astype(bf16).astype(f32)

    chunk = lax.broadcasted_iota(i32, (BATCH, depth), 0)
    place_in = lax.broadcasted_iota(i32, (BATCH, WIDTH), 0) * CHUNK + lax.broadcasted_iota(i32, (BATCH, WIDTH), 1)
    place_back = lax.broadcasted_iota(i32, (BATCH, WIDTH), 0) * CHUNK - lax.broadcasted_iota(i32, (BATCH, WIDTH), 1)

    def batch(l, first, origin):
        n = jnp.full((8, WIDTH), 2 * npoints[lat_rows[l]], i32).astype(f32)
        inverse = (1.0 / n)[0:1, 0:1]
        n = n[0:1, 0:1]
        center = (2 * CHUNK * (first + chunk) - 2 * origin + CHUNK - 1).astype(f32)
        k = wave_ref[...]
        weight = jnp.where(4.0 * k < n, jnp.where(k == 0.0, 1.0, 2.0), 0.0)
        all_cosine, all_sine = sincos(center * k, n, inverse)
        all_cosine, all_sine = all_cosine * weight, all_sine * weight
        for g in range(GROUPS):
            at = slice(g * rows, (g + 1) * rows)
            at_imag = slice(depth + g * rows, depth + (g + 1) * rows)
            cosine, sine = all_cosine[:, at], all_sine[:, at]
            for f in range(0, COLUMNS, 2):
                turned_real, turned_imag = [], []
                for i in (f, f + 1):
                    real, imag = parts[l, 0, i : i + 1, at], parts[l, 1, i : i + 1, at]
                    turned_real.append(real * cosine - imag * sine)
                    turned_imag.append(imag * cosine + real * sine)
                to = slice(f * BATCH, (f + 2) * BATCH)
                left[to, at] = jnp.concatenate(turned_real, axis=0).astype(bf16)
                left[to, at_imag] = jnp.concatenate(turned_imag, axis=0).astype(bf16)
        even = jnp.dot(left[:, 0:depth], table_ref[l, 0:depth], preferred_element_type=f32)
        odd = jnp.dot(left[:, depth : 2 * depth], table_ref[l, depth : 2 * depth], preferred_element_type=f32)
        before, after = even + odd, even - odd
        limit = origin - CHUNK * first
        keep_back = place_back + (WIDTH - 1) >= limit
        keep_in = place_in + WIDTH >= limit
        for f in range(COLUMNS):
            at = slice(f * BATCH, (f + 1) * BATCH)
            to = pl.ds(pl.multiple_of(f * chunks + first, 8), BATCH)
            line[to] = jnp.where(keep_back, before[at], line[to])
            to = pl.ds(pl.multiple_of((COLUMNS + f) * chunks + first, 8), BATCH)
            line[to] = jnp.where(keep_in, after[at], line[to])

    lane = lax.broadcasted_iota(i32, (COLUMNS, WIDTH), 1)
    for pair in range(2):
        n_a = npoints[lat_rows[2 * pair]]
        batches_a = lax.shift_right_arithmetic(n_a - 1, 11) + 1
        start_b = lax.shift_right_arithmetic(n_a, 11)

        def body(step, carry):
            second = step >= batches_a
            l = 2 * pair + jnp.where(second, 1, 0)
            first = BATCH * jnp.where(second, step - batches_a + start_b, step)
            batch(l, first, jnp.where(second, n_a, 0))
            return carry

        lax.fori_loop(0, batches_a + BATCHES - start_b, body, 0)
        back = slice(0, COLUMNS * chunks)
        line[back] = jnp.dot(line[back].astype(bf16), reverse_ref[...], preferred_element_type=f32)

        def tile_of(tile):
            return line[pl.ds((tile % 2) * COLUMNS * chunks + tile // 2, COLUMNS, chunks), :]

        for q in range(4):
            shift = (QUARTER * q) % WIDTH
            for i in range(QUARTER // WIDTH + 1):
                tile = QUARTER * q // WIDTH + i
                v = tile_of(tile)
                if shift:
                    v = jnp.where(
                        lane < WIDTH - shift,
                        pltpu.roll(v, WIDTH - shift, 1),
                        pltpu.roll(tile_of(tile + 1), WIDTH - shift, 1),
                    )
                if i < 10:
                    dense[q, COLUMNS * i : COLUMNS * i + COLUMNS] = v
                else:
                    dense[q, 200:208] = v[0:8]
                    dense[q, 200:208, 16:32] = v[8:16, 0:16]
                    dense[q, 200:204, 32:48] = v[16:20, 0:16]
            out_ref[4 * pair + q] = dense[q].astype(bf16)


def select_rows():
    table = np.zeros((GROUPS, 2 * ROWS, 128), np.float32)
    for g in range(GROUPS):
        for f in range(10):
            real, imag = g * ROWS + 2 * f, g * ROWS + 2 * f + 1
            table[g, f, real] = 1.0
            table[g, 10 + f, imag] = -1.0
            table[g, ROWS + f, imag] = 1.0
            table[g, ROWS + 10 + f, real] = 1.0
    return table.reshape(GROUPS * 2 * ROWS, 128).astype(jnp.bfloat16)


def synthesis(lat_rows, npoints, received, wave_line, tables, truncation):
    devices = received.shape[0]
    depth = GROUPS * TILES * devices
    reverse = np.eye(WIDTH)[::-1].astype(jnp.bfloat16)
    return pl.pallas_call(
        functools.partial(synthesis_kernel, float(truncation)),
        out_shape=jax.ShapeDtypeStruct((8, DENSE, WIDTH), bf16),
        in_specs=[pl.BlockSpec(memory_space=pltpu.SMEM)] * 2 + [VMEM_SPEC] * 5,
        out_specs=VMEM_SPEC,
        scratch_shapes=[
            pltpu.VMEM((devices * 4 * TILES, WIDTH), f32),
            pltpu.VMEM((4, 2, ROWS, depth), f32),
            pltpu.VMEM((BATCH * COLUMNS, 2 * depth), bf16),
            pltpu.VMEM((2 * COLUMNS * BATCH * BATCHES, WIDTH), f32),
            pltpu.VMEM((4, DENSE, WIDTH), f32),
        ],
        compiler_params=pltpu.CompilerParams(vmem_limit_bytes=16 << 20),
    )(lat_rows, npoints, received, wave_line, select_rows(), reverse, tables)


def place_kernel(in_ref, out_ref, dense, placed):
    for source in range(in_ref.shape[0]):
        dense[source] = in_ref[source].astype(f32)
        rest = dense[source, 200:208]
        rest = jnp.concatenate([rest, pltpu.roll(rest, WIDTH - 16, 1), pltpu.roll(rest, WIDTH - 32, 1)], axis=0)
        for kind in range(2):
            to = slice(10 * source, 10 * source + 10)
            for i in range(10):
                at = 20 * i + 10 * kind
                placed[kind, to, WIDTH * i : WIDTH * i + WIDTH] = dense[source, at : at + 10]
            placed[kind, to, 10 * WIDTH : QUARTER] = rest[10 * kind : 10 * kind + 10, 0:REST]
    out_ref[...] = placed[:, :, 0:QUARTER].astype(bf16)


def place(blocks):
    sources = blocks.shape[0]
    return pl.pallas_call(
        place_kernel,
        out_shape=jax.ShapeDtypeStruct((2, 10 * sources, QUARTER), bf16),
        in_specs=[VMEM_SPEC],
        out_specs=VMEM_SPEC,
        scratch_shapes=[
            pltpu.VMEM((sources, DENSE, WIDTH), f32),
            pltpu.VMEM((2, 10 * sources, 11 * WIDTH), f32),
        ],
        compiler_params=pltpu.CompilerParams(vmem_limit_bytes=8 << 20),
    )(blocks)


def wave_line_of(index, truncation):
    low = jnp.transpose(index[:, 0, 0:10])
    both = jnp.stack([low, truncation - low], axis=1)
    both = both.reshape(TILES, GROUPS, index.shape[0])
    return jnp.transpose(both, (1, 0, 2)).reshape(1, -1)


def on_device(spectral, legendre, wave_pairs, npoints, lat_rows):
    truncation = legendre.shape[1] - 2
    devices = lax.axis_size("wave")
    index = lax.all_to_all(announcement(wave_pairs, lat_rows, devices), "wave", 0, 0, tiled=True)
    sums = legendre_sums(wave_pairs, spectral, legendre)
    ordered = order_latitudes(index, sums)
    received = lax.all_to_all(ordered, "wave", 0, 0, tiled=True)
    tables = fourier_tables(lat_rows, npoints, index, truncation)
    wave_line = wave_line_of(index, float(truncation))
    blocks = synthesis(lat_rows, npoints, received, wave_line, tables, truncation)
    return place(lax.all_to_all(blocks, "field", 0, 0, tiled=True))


def solution(mesh):
    placed = (P("wave", None, None, "field"), P("wave", None, None), P("wave"), P(), P("wave"))
    return jax.shard_map(
        on_device,
        mesh=mesh,
        in_specs=placed,
        out_specs=P(None, None, ("wave", "field")),
        check_vma=False,
    )
```

```python
import functools

import jax
import jax.numpy as jnp
import numpy as np
from jax import lax
from jax.experimental import pallas as pl
from jax.experimental.pallas import tpu as pltpu
from jax.sharding import PartitionSpec as P

ROW_PAIR = 5156
QUARTER = ROW_PAIR // 4
CHUNK = 256
GROUPS = 5
TILES = 4
ROWS = 24
SIN = (6.283184915155849, -41.3415888250942, 81.59992747560547, -76.6142661520567, 41.34181133252104, -12.469328879159221)
COS = (0.9999992080920543, -19.73897953618229, 64.92862553583919, -85.27120644254374, 58.78833787867872, -21.067254412050286)
f32, bf16, i32 = jnp.float32, jnp.bfloat16, jnp.int32
VMEM_SPEC = pl.BlockSpec(memory_space=pltpu.VMEM)


def legendre_kernel(truncation, waves, spec_hbm, leg_hbm, out_ref, spec_ref, leg_ref, coeffs, spec_sems, leg_sems):
    rows = truncation + 2
    slots, fields = spec_ref.shape[0], spec_ref.shape[1]
    main = rows - 1

    def copies(slot):
        return (
            pltpu.make_async_copy(spec_hbm.at[slot], spec_ref.at[slot], spec_sems.at[slot]),
            pltpu.make_async_copy(leg_hbm.at[slot], leg_ref.at[slot], leg_sems.at[slot]),
        )

    for slot in range(slots):
        for copy in copies(slot):
            copy.start()
    coeffs[...] = jnp.zeros_like(coeffs)

    def body(slot, carry):
        for copy in copies(slot):
            copy.wait()
        for field in range(fields):
            coeffs[2 * field : 2 * field + 2, 0:rows] = spec_ref[slot, field]
        split = truncation + 1 - waves[slot]
        row = lax.broadcasted_iota(i32, (1, rows), 1)
        low = row < split
        offset = jnp.where(low, row, row - split)
        sign = jnp.where(offset % 2 == 0, 1.0, -1.0).astype(f32)
        low = jnp.where(low, 1.0, 0.0).astype(f32)
        high = 1.0 - low
        values = coeffs[:, 0:rows]
        stacked = jnp.concatenate([values * mask for mask in (low, low * sign, high, high * sign)], axis=0)
        stacked = stacked.astype(bf16)
        sums = jnp.dot(stacked[:, 0:main], leg_ref[slot, 0:main, :], preferred_element_type=f32)
        last = stacked[:, main:rows].astype(f32) * leg_ref[slot, main:rows, :].astype(f32)
        sums = sums + last
        for half in range(2):
            for side in range(2):
                at = (2 * half + side) * ROWS
                out_ref[2 * slot + half, :, 128 * side : 128 * side + 128] = sums[at : at + ROWS, :]
        return carry

    lax.fori_loop(0, slots, body, 0)


def legendre_sums(wave_pairs, spectral, legendre):
    slots, rows, northern = legendre.shape
    fields = spectral.shape[3]
    parts = pltpu.with_memory_space_constraint(jnp.transpose(spectral, (0, 3, 2, 1)), pltpu.HBM)
    legendre = pltpu.with_memory_space_constraint(legendre, pltpu.HBM)
    return pl.pallas_call(
        functools.partial(legendre_kernel, rows - 2),
        out_shape=pltpu.VMEM((2 * slots, ROWS, 2 * northern), f32),
        in_specs=[pl.BlockSpec(memory_space=pltpu.SMEM)] + [pl.BlockSpec(memory_space=pltpu.HBM)] * 2,
        out_specs=VMEM_SPEC,
        scratch_shapes=[
            pltpu.VMEM((slots, fields, 2, rows), f32),
            pltpu.VMEM((slots, rows, northern), bf16),
            pltpu.VMEM((ROWS, 1408), f32),
            pltpu.SemaphoreType.DMA((slots,)),
            pltpu.SemaphoreType.DMA((slots,)),
        ],
        compiler_params=pltpu.CompilerParams(vmem_limit_bytes=16 << 20),
    )(pltpu.with_memory_space_constraint(wave_pairs, pltpu.HBM), parts, legendre)


def announce_kernel(waves, lats, out_ref):
    lane = lax.broadcasted_iota(i32, (1, 128), 1)
    row = jnp.zeros((1, 128), i32)
    for i in range(14):
        row = jnp.where(lane == i, waves[i] if i < 10 else lats[i - 10], row)
    out_ref[...] = jnp.broadcast_to(row.astype(f32).reshape(1, 1, 128), out_ref.shape)


def announcement(wave_pairs, lat_rows, devices):
    return pl.pallas_call(
        announce_kernel,
        out_shape=jax.ShapeDtypeStruct((devices, 1, 128), f32),
        in_specs=[pl.BlockSpec(memory_space=pltpu.SMEM)] * 2,
        out_specs=VMEM_SPEC,
        compiler_params=pltpu.CompilerParams(vmem_limit_bytes=1 << 20),
    )(*(pltpu.with_memory_space_constraint(x, pltpu.HBM) for x in (wave_pairs, lat_rows)))


def order_kernel(index_ref, sums_ref, out_ref, scratch):
    devices, lats = index_ref.shape[0], sums_ref.shape[2]
    index = index_ref[:, 0, :]
    lane = lax.broadcasted_iota(i32, (devices, lats), 1).astype(f32)
    onehot = jnp.concatenate(
        [jnp.where(index[:, 10 + j : 11 + j] == lane, 1.0, 0.0) for j in range(4)], axis=0
    ).astype(bf16)
    for t in range(TILES):
        part = sums_ref[GROUPS * t : GROUPS * (t + 1)].reshape(GROUPS * ROWS, lats)
        part = jnp.concatenate([part, jnp.zeros((128 - GROUPS * ROWS, lats), f32)], axis=0).astype(bf16)
        picked = lax.dot_general(onehot, part, (((1,), (1,)), ((), ())), preferred_element_type=f32)
        for j in range(4):
            scratch[pl.ds(j * TILES + t, devices, 4 * TILES), :] = picked[devices * j : devices * (j + 1), :]
    out_ref[...] = scratch[...].reshape(out_ref.shape).astype(bf16)


def order_latitudes(index, sums):
    devices = index.shape[0]
    return pl.pallas_call(
        order_kernel,
        out_shape=jax.ShapeDtypeStruct((devices, 4 * TILES, 128), bf16),
        in_specs=[VMEM_SPEC] * 2,
        out_specs=VMEM_SPEC,
        scratch_shapes=[pltpu.VMEM((devices * 4 * TILES, 128), f32)],
        compiler_params=pltpu.CompilerParams(vmem_limit_bytes=8 << 20),
    )(index, sums)


def poly(coefficients, y):
    total = jnp.full_like(y, coefficients[-1])
    for c in coefficients[-2::-1]:
        total = total * y + c
    return total


def sincos(product, n, inverse):
    turns = jnp.floor(product * inverse + 0.5)
    f = (product - turns * n) * inverse
    y = f * f
    return poly(COS, y), poly(SIN, y) * f


BLOCK = 128


def table_kernel(truncation, lat_rows, npoints, index_ref, out_ref, waves):
    l = pl.program_id(0)
    devices = index_ref.shape[0]
    depth = GROUPS * TILES * devices

    @pl.when(l == 0)
    def _():
        index = index_ref[:, 0, :]
        for g in range(GROUPS):
            for t in range(TILES):
                ph = GROUPS * t + g
                column = index[:, ph // 2 : ph // 2 + 1]
                if ph % 2:
                    column = truncation - column
                at = devices * (TILES * g + t)
                waves[at : at + devices, :] = jnp.broadcast_to(column, (devices, 128))

    odd = (2 * lax.broadcasted_iota(i32, (BLOCK, 128), 1) + 1).astype(f32)
    n = jnp.full((8, 128), 2 * npoints[lat_rows[l]], i32).astype(f32)
    inverse = (1.0 / n)[0:1]
    n = n[0:1]

    def rows_block(r, carry):
        at = pl.multiple_of(r * BLOCK, BLOCK)
        cosine, sine = sincos(waves[pl.ds(at, BLOCK), :] * odd, n, inverse)
        out_ref[0, pl.ds(at, BLOCK), :] = cosine.astype(bf16)
        out_ref[0, pl.ds(depth + at, BLOCK), :] = sine.astype(bf16)
        return carry

    lax.fori_loop(0, depth // BLOCK, rows_block, 0)


def fourier_tables(lat_rows, npoints, index, truncation):
    devices = index.shape[0]
    depth = GROUPS * TILES * devices
    return pl.pallas_call(
        functools.partial(table_kernel, float(truncation)),
        out_shape=pltpu.VMEM((4, 2 * depth, CHUNK // 2), bf16),
        grid_spec=pltpu.PrefetchScalarGridSpec(
            num_scalar_prefetch=2,
            grid=(4,),
            in_specs=[VMEM_SPEC],
            out_specs=pl.BlockSpec((1, 2 * depth, CHUNK // 2), lambda l, a, b: (l, 0, 0)),
            scratch_shapes=[pltpu.VMEM((depth, 128), f32)],
        ),
        compiler_params=pltpu.CompilerParams(vmem_limit_bytes=8 << 20),
    )(lat_rows, npoints, index)


BATCH = 8
BATCHES = 3
WIDTH = 128
COLUMNS = 20
DENSE = 208
REST = QUARTER - 10 * WIDTH


def synthesis_kernel(
    truncation, lat_rows, npoints, got_ref, wave_ref, select_ref, reverse_ref, table_ref, out_ref, got, parts, left_0, left_1, line_0, line_1, dense
):
    devices = got_ref.shape[0]
    rows = TILES * devices
    depth = GROUPS * rows
    chunks = BATCH * BATCHES
    got[...] = got_ref[...].reshape(devices * 4 * TILES, WIDTH).astype(f32)
    for l in range(4):
        stacked = jnp.concatenate(
            [got[pl.ds(l * TILES + t, devices, 4 * TILES), :] for t in range(TILES)], axis=0
        ).astype(bf16)
        both = lax.dot_general(select_ref[...], stacked, (((1,), (1,)), ((), ())), preferred_element_type=f32)
        for g in range(GROUPS):
            at = slice(g * rows, (g + 1) * rows)
            row = lax.broadcasted_iota(i32, (ROWS, rows), 0)
            scale = jnp.where(row < 10, 1.0, jnp.broadcast_to(wave_ref[:, at] / truncation, (ROWS, rows)))
            for c in range(2):
                part = both[ROWS * (2 * g + c) : ROWS * (2 * g + c + 1)] * scale
                parts[l, c, :, at] = part.astype(bf16).astype(f32)

    chunk = lax.broadcasted_iota(i32, (BATCH, depth), 0)
    place_in = lax.broadcasted_iota(i32, (BATCH, WIDTH), 0) * CHUNK + lax.broadcasted_iota(i32, (BATCH, WIDTH), 1)
    place_back = lax.broadcasted_iota(i32, (BATCH, WIDTH), 0) * CHUNK - lax.broadcasted_iota(i32, (BATCH, WIDTH), 1)

    lefts, lines = (left_0, left_1), (line_0, line_1)

    def rotate(left, l, first, origin):
        n = jnp.full((8, WIDTH), 2 * npoints[lat_rows[l]], i32).astype(f32)
        inverse = (1.0 / n)[0:1, 0:1]
        n = n[0:1, 0:1]
        center = (2 * CHUNK * (first + chunk) - 2 * origin + CHUNK - 1).astype(f32)
        k = wave_ref[...]
        weight = jnp.where(4.0 * k < n, jnp.where(k == 0.0, 1.0, 2.0), 0.0)
        all_cosine, all_sine = sincos(center * k, n, inverse)
        all_cosine, all_sine = all_cosine * weight, all_sine * weight
        for g in range(GROUPS):
            at = slice(g * rows, (g + 1) * rows)
            at_imag = slice(depth + g * rows, depth + (g + 1) * rows)
            cosine, sine = all_cosine[:, at], all_sine[:, at]
            for f in range(0, COLUMNS, 2):
                turned_real, turned_imag = [], []
                for i in (f, f + 1):
                    real, imag = parts[l, 0, i : i + 1, at], parts[l, 1, i : i + 1, at]
                    turned_real.append(real * cosine - imag * sine)
                    turned_imag.append(imag * cosine + real * sine)
                to = slice(f * BATCH, (f + 2) * BATCH)
                left[to, at] = jnp.concatenate(turned_real, axis=0).astype(bf16)
                left[to, at_imag] = jnp.concatenate(turned_imag, axis=0).astype(bf16)

    def multiply(left, line, l, first, origin):
        even = jnp.dot(left[:, 0:depth], table_ref[l, 0:depth], preferred_element_type=f32)
        odd = jnp.dot(left[:, depth : 2 * depth], table_ref[l, depth : 2 * depth], preferred_element_type=f32)
        before, after = even + odd, even - odd
        limit = origin - CHUNK * first
        keep_back = place_back + (WIDTH - 1) >= limit
        keep_in = place_in + WIDTH >= limit
        for f in range(COLUMNS):
            at = slice(f * BATCH, (f + 1) * BATCH)
            to = pl.ds(pl.multiple_of(f * chunks + first, 8), BATCH)
            line[to] = jnp.where(keep_back, before[at], line[to])
            to = pl.ds(pl.multiple_of((COLUMNS + f) * chunks + first, 8), BATCH)
            line[to] = jnp.where(keep_in, after[at], line[to])

    def body(step, carry):
        at = []
        for pair in range(2):
            n_a = npoints[lat_rows[2 * pair]]
            batches_a = lax.shift_right_arithmetic(n_a - 1, 11) + 1
            start_b = lax.shift_right_arithmetic(n_a, 11)
            second = step >= batches_a
            index = jnp.where(second, jnp.minimum(step - batches_a + start_b, BATCHES - 1), step)
            at.append((2 * pair + jnp.where(second, 1, 0), BATCH * index, jnp.where(second, n_a, 0)))
        for pair in range(2):
            rotate(lefts[pair], *at[pair])
        for pair in range(2):
            multiply(lefts[pair], lines[pair], *at[pair])
        return carry

    lax.fori_loop(0, BATCHES + 1, body, 0, unroll=True)
    lane = lax.broadcasted_iota(i32, (COLUMNS, WIDTH), 1)
    for pair in range(2):
        line = lines[pair]
        back = slice(0, COLUMNS * chunks)
        line[back] = jnp.dot(line[back].astype(bf16), reverse_ref[...], preferred_element_type=f32)

        def tile_of(tile, line=line):
            return line[pl.ds((tile % 2) * COLUMNS * chunks + tile // 2, COLUMNS, chunks), :]

        for q in range(4):
            shift = (QUARTER * q) % WIDTH
            for i in range(QUARTER // WIDTH + 1):
                tile = QUARTER * q // WIDTH + i
                v = tile_of(tile)
                if shift:
                    v = jnp.where(
                        lane < WIDTH - shift,
                        pltpu.roll(v, WIDTH - shift, 1),
                        pltpu.roll(tile_of(tile + 1), WIDTH - shift, 1),
                    )
                if i < 10:
                    dense[q, COLUMNS * i : COLUMNS * i + COLUMNS] = v
                else:
                    dense[q, 200:208] = v[0:8]
                    dense[q, 200:208, 16:32] = v[8:16, 0:16]
                    dense[q, 200:204, 32:48] = v[16:20, 0:16]
            out_ref[4 * pair + q] = dense[q].astype(bf16)


def select_rows():
    table = np.zeros((GROUPS, 2 * ROWS, 128), np.float32)
    for g in range(GROUPS):
        for f in range(10):
            real, imag = g * ROWS + 2 * f, g * ROWS + 2 * f + 1
            table[g, f, real] = 1.0
            table[g, 10 + f, imag] = -1.0
            table[g, ROWS + f, imag] = 1.0
            table[g, ROWS + 10 + f, real] = 1.0
    return table.reshape(GROUPS * 2 * ROWS, 128).astype(jnp.bfloat16)


def synthesis(lat_rows, npoints, received, wave_line, tables, truncation):
    devices = received.shape[0]
    depth = GROUPS * TILES * devices
    reverse = np.eye(WIDTH)[::-1].astype(jnp.bfloat16)
    return pl.pallas_call(
        functools.partial(synthesis_kernel, float(truncation)),
        out_shape=jax.ShapeDtypeStruct((8, DENSE, WIDTH), bf16),
        in_specs=[pl.BlockSpec(memory_space=pltpu.SMEM)] * 2 + [VMEM_SPEC] * 5,
        out_specs=VMEM_SPEC,
        scratch_shapes=[
            pltpu.VMEM((devices * 4 * TILES, WIDTH), f32),
            pltpu.VMEM((4, 2, ROWS, depth), f32),
            pltpu.VMEM((BATCH * COLUMNS, 2 * depth), bf16),
            pltpu.VMEM((BATCH * COLUMNS, 2 * depth), bf16),
            pltpu.VMEM((2 * COLUMNS * BATCH * BATCHES, WIDTH), f32),
            pltpu.VMEM((2 * COLUMNS * BATCH * BATCHES, WIDTH), f32),
            pltpu.VMEM((4, DENSE, WIDTH), f32),
        ],
        compiler_params=pltpu.CompilerParams(vmem_limit_bytes=16 << 20),
    )(lat_rows, npoints, received, wave_line, select_rows(), reverse, tables)


def place_kernel(in_ref, out_ref, dense, placed):
    for source in range(in_ref.shape[0]):
        dense[source] = in_ref[source].astype(f32)
        rest = dense[source, 200:208]
        rest = jnp.concatenate([rest, pltpu.roll(rest, WIDTH - 16, 1), pltpu.roll(rest, WIDTH - 32, 1)], axis=0)
        for kind in range(2):
            to = slice(10 * source, 10 * source + 10)
            for i in range(10):
                at = 20 * i + 10 * kind
                placed[kind, to, WIDTH * i : WIDTH * i + WIDTH] = dense[source, at : at + 10]
            placed[kind, to, 10 * WIDTH : QUARTER] = rest[10 * kind : 10 * kind + 10, 0:REST]
    out_ref[...] = placed[:, :, 0:QUARTER].astype(bf16)


def place(blocks):
    sources = blocks.shape[0]
    return pl.pallas_call(
        place_kernel,
        out_shape=jax.ShapeDtypeStruct((2, 10 * sources, QUARTER), bf16),
        in_specs=[VMEM_SPEC],
        out_specs=VMEM_SPEC,
        scratch_shapes=[
            pltpu.VMEM((sources, DENSE, WIDTH), f32),
            pltpu.VMEM((2, 10 * sources, 11 * WIDTH), f32),
        ],
        compiler_params=pltpu.CompilerParams(vmem_limit_bytes=8 << 20),
    )(blocks)


def wave_line_of(index, truncation):
    low = jnp.transpose(index[:, 0, 0:10])
    both = jnp.stack([low, truncation - low], axis=1)
    both = both.reshape(TILES, GROUPS, index.shape[0])
    return jnp.transpose(both, (1, 0, 2)).reshape(1, -1)


def on_device(spectral, legendre, wave_pairs, npoints, lat_rows):
    truncation = legendre.shape[1] - 2
    devices = lax.axis_size("wave")
    index = lax.all_to_all(announcement(wave_pairs, lat_rows, devices), "wave", 0, 0, tiled=True)
    sums = legendre_sums(wave_pairs, spectral, legendre)
    ordered = order_latitudes(index, sums)
    received = lax.all_to_all(ordered, "wave", 0, 0, tiled=True)
    tables = fourier_tables(lat_rows, npoints, index, truncation)
    wave_line = wave_line_of(index, float(truncation))
    blocks = synthesis(lat_rows, npoints, received, wave_line, tables, truncation)
    return place(lax.all_to_all(blocks, "field", 0, 0, tiled=True))


def solution(mesh):
    placed = (P("wave", None, None, "field"), P("wave", None, None), P("wave"), P(), P("wave"))
    return jax.shard_map(
        on_device,
        mesh=mesh,
        in_specs=placed,
        out_specs=P(None, None, ("wave", "field")),
        check_vma=False,
    )
```

```python
import functools

import jax
import jax.numpy as jnp
import numpy as np
from jax import lax
from jax.experimental import pallas as pl
from jax.experimental.pallas import tpu as pltpu
from jax.sharding import PartitionSpec as P

ROW_PAIR = 5156
QUARTER = ROW_PAIR // 4
CHUNK = 256
GROUPS = 5
TILES = 4
ROWS = 24
SIN = (6.283184915155849, -41.3415888250942, 81.59992747560547, -76.6142661520567, 41.34181133252104, -12.469328879159221)
COS = (0.9999992080920543, -19.73897953618229, 64.92862553583919, -85.27120644254374, 58.78833787867872, -21.067254412050286)
f32, bf16, i32 = jnp.float32, jnp.bfloat16, jnp.int32
VMEM_SPEC = pl.BlockSpec(memory_space=pltpu.VMEM)


def legendre_kernel(truncation, waves, spec_hbm, leg_hbm, out_ref, spec_ref, leg_ref, coeffs, spec_sems, leg_sems):
    rows = truncation + 2
    slots, fields = spec_ref.shape[0], spec_ref.shape[1]
    main = rows - 1

    def copies(slot):
        return (
            pltpu.make_async_copy(spec_hbm.at[slot], spec_ref.at[slot], spec_sems.at[slot]),
            pltpu.make_async_copy(leg_hbm.at[slot], leg_ref.at[slot], leg_sems.at[slot]),
        )

    for slot in range(slots):
        for copy in copies(slot):
            copy.start()
    coeffs[...] = jnp.zeros_like(coeffs)

    def body(slot, carry):
        for copy in copies(slot):
            copy.wait()
        for field in range(fields):
            coeffs[2 * field : 2 * field + 2, 0:rows] = spec_ref[slot, field]
        split = truncation + 1 - waves[slot]
        row = lax.broadcasted_iota(i32, (1, rows), 1)
        low = row < split
        offset = jnp.where(low, row, row - split)
        sign = jnp.where(offset % 2 == 0, 1.0, -1.0).astype(f32)
        low = jnp.where(low, 1.0, 0.0).astype(f32)
        high = 1.0 - low
        values = coeffs[:, 0:rows]
        stacked = jnp.concatenate([values * mask for mask in (low, low * sign, high, high * sign)], axis=0)
        stacked = stacked.astype(bf16)
        sums = jnp.dot(stacked[:, 0:main], leg_ref[slot, 0:main, :], preferred_element_type=f32)
        last = stacked[:, main:rows].astype(f32) * leg_ref[slot, main:rows, :].astype(f32)
        sums = sums + last
        for half in range(2):
            for side in range(2):
                at = (2 * half + side) * ROWS
                out_ref[2 * slot + half, :, 128 * side : 128 * side + 128] = sums[at : at + ROWS, :]
        return carry

    lax.fori_loop(0, slots, body, 0)


def legendre_sums(wave_pairs, spectral, legendre):
    slots, rows, northern = legendre.shape
    fields = spectral.shape[3]
    parts = pltpu.with_memory_space_constraint(jnp.transpose(spectral, (0, 3, 2, 1)), pltpu.HBM)
    legendre = pltpu.with_memory_space_constraint(legendre, pltpu.HBM)
    return pl.pallas_call(
        functools.partial(legendre_kernel, rows - 2),
        out_shape=pltpu.VMEM((2 * slots, ROWS, 2 * northern), f32),
        in_specs=[pl.BlockSpec(memory_space=pltpu.SMEM)] + [pl.BlockSpec(memory_space=pltpu.HBM)] * 2,
        out_specs=VMEM_SPEC,
        scratch_shapes=[
            pltpu.VMEM((slots, fields, 2, rows), f32),
            pltpu.VMEM((slots, rows, northern), bf16),
            pltpu.VMEM((ROWS, 1408), f32),
            pltpu.SemaphoreType.DMA((slots,)),
            pltpu.SemaphoreType.DMA((slots,)),
        ],
        compiler_params=pltpu.CompilerParams(vmem_limit_bytes=16 << 20),
    )(pltpu.with_memory_space_constraint(wave_pairs, pltpu.HBM), parts, legendre)


def announce_kernel(waves, lats, out_ref):
    lane = lax.broadcasted_iota(i32, (1, 128), 1)
    row = jnp.zeros((1, 128), i32)
    for i in range(14):
        row = jnp.where(lane == i, waves[i] if i < 10 else lats[i - 10], row)
    out_ref[...] = jnp.broadcast_to(row.astype(f32).reshape(1, 1, 128), out_ref.shape)


def announcement(wave_pairs, lat_rows, devices):
    return pl.pallas_call(
        announce_kernel,
        out_shape=jax.ShapeDtypeStruct((devices, 1, 128), f32),
        in_specs=[pl.BlockSpec(memory_space=pltpu.SMEM)] * 2,
        out_specs=VMEM_SPEC,
        compiler_params=pltpu.CompilerParams(vmem_limit_bytes=1 << 20),
    )(*(pltpu.with_memory_space_constraint(x, pltpu.HBM) for x in (wave_pairs, lat_rows)))


def order_kernel(index_ref, sums_ref, out_ref, scratch):
    devices, lats = index_ref.shape[0], sums_ref.shape[2]
    index = index_ref[:, 0, :]
    lane = lax.broadcasted_iota(i32, (devices, lats), 1).astype(f32)
    onehot = jnp.concatenate(
        [jnp.where(index[:, 10 + j : 11 + j] == lane, 1.0, 0.0) for j in range(4)], axis=0
    ).astype(bf16)
    for t in range(TILES):
        part = sums_ref[GROUPS * t : GROUPS * (t + 1)].reshape(GROUPS * ROWS, lats)
        part = jnp.concatenate([part, jnp.zeros((128 - GROUPS * ROWS, lats), f32)], axis=0).astype(bf16)
        picked = lax.dot_general(onehot, part, (((1,), (1,)), ((), ())), preferred_element_type=f32)
        for j in range(4):
            scratch[pl.ds(j * TILES + t, devices, 4 * TILES), :] = picked[devices * j : devices * (j + 1), :]
    out_ref[...] = scratch[...].reshape(out_ref.shape).astype(bf16)


def order_latitudes(index, sums):
    devices = index.shape[0]
    return pl.pallas_call(
        order_kernel,
        out_shape=jax.ShapeDtypeStruct((devices, 4 * TILES, 128), bf16),
        in_specs=[VMEM_SPEC] * 2,
        out_specs=VMEM_SPEC,
        scratch_shapes=[pltpu.VMEM((devices * 4 * TILES, 128), f32)],
        compiler_params=pltpu.CompilerParams(vmem_limit_bytes=8 << 20),
    )(index, sums)


def poly(coefficients, y):
    total = jnp.full_like(y, coefficients[-1])
    for c in coefficients[-2::-1]:
        total = total * y + c
    return total


def sincos(product, n, inverse):
    turns = jnp.floor(product * inverse + 0.5)
    f = (product - turns * n) * inverse
    y = f * f
    return poly(COS, y), poly(SIN, y) * f


BLOCK = 128


def table_kernel(truncation, lat_rows, npoints, index_ref, out_ref, points_ref, waves):
    l = pl.program_id(0)
    devices = index_ref.shape[0]
    depth = GROUPS * TILES * devices

    @pl.when(l == 0)
    def _():
        index = index_ref[:, 0, :]
        for g in range(GROUPS):
            for t in range(TILES):
                ph = GROUPS * t + g
                column = index[:, ph // 2 : ph // 2 + 1]
                if ph % 2:
                    column = truncation - column
                at = devices * (TILES * g + t)
                waves[at : at + devices, :] = jnp.broadcast_to(column, (devices, 128))

    points_ref[l] = npoints[lat_rows[l]]
    odd = (2 * lax.broadcasted_iota(i32, (BLOCK, 128), 1) + 1).astype(f32)
    n = jnp.full((8, 128), 2 * npoints[lat_rows[l]], i32).astype(f32)
    inverse = (1.0 / n)[0:1]
    n = n[0:1]

    def rows_block(r, carry):
        at = pl.multiple_of(r * BLOCK, BLOCK)
        cosine, sine = sincos(waves[pl.ds(at, BLOCK), :] * odd, n, inverse)
        out_ref[0, pl.ds(at, BLOCK), :] = cosine.astype(bf16)
        out_ref[0, pl.ds(depth + at, BLOCK), :] = sine.astype(bf16)
        return carry

    lax.fori_loop(0, depth // BLOCK, rows_block, 0)


def fourier_tables(lat_rows, npoints, index, truncation):
    devices = index.shape[0]
    depth = GROUPS * TILES * devices
    return pl.pallas_call(
        functools.partial(table_kernel, float(truncation)),
        out_shape=(pltpu.VMEM((4, 2 * depth, CHUNK // 2), bf16), jax.ShapeDtypeStruct((4,), i32)),
        grid_spec=pltpu.PrefetchScalarGridSpec(
            num_scalar_prefetch=2,
            grid=(4,),
            in_specs=[VMEM_SPEC],
            out_specs=(
                pl.BlockSpec((1, 2 * depth, CHUNK // 2), lambda l, a, b: (l, 0, 0)),
                pl.BlockSpec(memory_space=pltpu.SMEM),
            ),
            scratch_shapes=[pltpu.VMEM((depth, 128), f32)],
        ),
        compiler_params=pltpu.CompilerParams(vmem_limit_bytes=8 << 20),
    )(lat_rows, npoints, index)


BATCH = 8
BATCHES = 3
WIDTH = 128
COLUMNS = 20
DENSE = 208
REST = QUARTER - 10 * WIDTH


def synthesis_kernel(
    truncation, points, got_ref, wave_ref, select_ref, reverse_ref, table_ref, out_ref, got, parts, left_0, left_1, line_0, line_1, dense
):
    devices = got_ref.shape[0]
    rows = TILES * devices
    depth = GROUPS * rows
    chunks = BATCH * BATCHES
    got[...] = got_ref[...].reshape(devices * 4 * TILES, WIDTH).astype(f32)
    for l in range(4):
        stacked = jnp.concatenate(
            [got[pl.ds(l * TILES + t, devices, 4 * TILES), :] for t in range(TILES)], axis=0
        ).astype(bf16)
        both = lax.dot_general(select_ref[...], stacked, (((1,), (1,)), ((), ())), preferred_element_type=f32)
        for g in range(GROUPS):
            at = slice(g * rows, (g + 1) * rows)
            row = lax.broadcasted_iota(i32, (ROWS, rows), 0)
            scale = jnp.where(row < 10, 1.0, jnp.broadcast_to(wave_ref[:, at] / truncation, (ROWS, rows)))
            for c in range(2):
                part = both[ROWS * (2 * g + c) : ROWS * (2 * g + c + 1)] * scale
                parts[l, c, :, at] = part.astype(bf16).astype(f32)

    chunk = lax.broadcasted_iota(i32, (BATCH, depth), 0)
    place_in = lax.broadcasted_iota(i32, (BATCH, WIDTH), 0) * CHUNK + lax.broadcasted_iota(i32, (BATCH, WIDTH), 1)
    place_back = lax.broadcasted_iota(i32, (BATCH, WIDTH), 0) * CHUNK - lax.broadcasted_iota(i32, (BATCH, WIDTH), 1)

    lefts, lines = (left_0, left_1), (line_0, line_1)

    def rotate(left, l, first, origin):
        n = jnp.full((8, WIDTH), 2 * points[l], i32).astype(f32)
        inverse = (1.0 / n)[0:1, 0:1]
        n = n[0:1, 0:1]
        center = (2 * CHUNK * (first + chunk) - 2 * origin + CHUNK - 1).astype(f32)
        k = wave_ref[...]
        weight = jnp.where(4.0 * k < n, jnp.where(k == 0.0, 1.0, 2.0), 0.0)
        all_cosine, all_sine = sincos(center * k, n, inverse)
        all_cosine, all_sine = all_cosine * weight, all_sine * weight
        for g in range(GROUPS):
            at = slice(g * rows, (g + 1) * rows)
            at_imag = slice(depth + g * rows, depth + (g + 1) * rows)
            cosine, sine = all_cosine[:, at], all_sine[:, at]
            for f in range(0, COLUMNS, 2):
                turned_real, turned_imag = [], []
                for i in (f, f + 1):
                    real, imag = parts[l, 0, i : i + 1, at], parts[l, 1, i : i + 1, at]
                    turned_real.append(real * cosine - imag * sine)
                    turned_imag.append(imag * cosine + real * sine)
                to = slice(f * BATCH, (f + 2) * BATCH)
                left[to, at] = jnp.concatenate(turned_real, axis=0).astype(bf16)
                left[to, at_imag] = jnp.concatenate(turned_imag, axis=0).astype(bf16)

    def multiply(left, line, l, first, origin):
        even = jnp.dot(left[:, 0:depth], table_ref[l, 0:depth], preferred_element_type=f32)
        odd = jnp.dot(left[:, depth : 2 * depth], table_ref[l, depth : 2 * depth], preferred_element_type=f32)
        before, after = even + odd, even - odd
        limit = origin - CHUNK * first
        keep_back = place_back + (WIDTH - 1) >= limit
        keep_in = place_in + WIDTH >= limit
        for f in range(COLUMNS):
            at = slice(f * BATCH, (f + 1) * BATCH)
            to = pl.ds(pl.multiple_of(f * chunks + first, 8), BATCH)
            line[to] = jnp.where(keep_back, before[at], line[to])
            to = pl.ds(pl.multiple_of((COLUMNS + f) * chunks + first, 8), BATCH)
            line[to] = jnp.where(keep_in, after[at], line[to])

    def body(step, carry):
        at = []
        for pair in range(2):
            n_a = points[2 * pair]
            batches_a = lax.shift_right_arithmetic(n_a - 1, 11) + 1
            start_b = lax.shift_right_arithmetic(n_a, 11)
            second = step >= batches_a
            index = jnp.where(second, jnp.minimum(step - batches_a + start_b, BATCHES - 1), step)
            at.append((2 * pair + jnp.where(second, 1, 0), BATCH * index, jnp.where(second, n_a, 0)))
        for pair in range(2):
            rotate(lefts[pair], *at[pair])
        for pair in range(2):
            multiply(lefts[pair], lines[pair], *at[pair])
        return carry

    lax.fori_loop(0, BATCHES + 1, body, 0, unroll=True)
    lane = lax.broadcasted_iota(i32, (COLUMNS, WIDTH), 1)
    for pair in range(2):
        line = lines[pair]
        back = slice(0, COLUMNS * chunks)
        line[back] = jnp.dot(line[back].astype(bf16), reverse_ref[...], preferred_element_type=f32)

        def tile_of(tile, line=line):
            return line[pl.ds((tile % 2) * COLUMNS * chunks + tile // 2, COLUMNS, chunks), :]

        for q in range(4):
            shift = (QUARTER * q) % WIDTH
            first = QUARTER * q // WIDTH
            ahead = tile_of(first)
            if shift:
                ahead = pltpu.roll(ahead, WIDTH - shift, 1)
            for i in range(QUARTER // WIDTH + 1):
                v = ahead
                if shift or i < QUARTER // WIDTH:
                    ahead = tile_of(first + i + 1)
                if shift:
                    ahead = pltpu.roll(ahead, WIDTH - shift, 1)
                    v = jnp.where(lane < WIDTH - shift, v, ahead)
                if i < 10:
                    dense[q, COLUMNS * i : COLUMNS * i + COLUMNS] = v
                else:
                    dense[q, 200:208] = v[0:8]
                    dense[q, 200:208, 16:32] = v[8:16, 0:16]
                    dense[q, 200:204, 32:48] = v[16:20, 0:16]
            out_ref[4 * pair + q] = dense[q].astype(bf16)


def select_rows():
    table = np.zeros((GROUPS, 2 * ROWS, 128), np.float32)
    for g in range(GROUPS):
        for f in range(10):
            real, imag = g * ROWS + 2 * f, g * ROWS + 2 * f + 1
            table[g, f, real] = 1.0
            table[g, 10 + f, imag] = -1.0
            table[g, ROWS + f, imag] = 1.0
            table[g, ROWS + 10 + f, real] = 1.0
    return table.reshape(GROUPS * 2 * ROWS, 128).astype(jnp.bfloat16)


def synthesis(points, received, wave_line, tables, truncation):
    devices = received.shape[0]
    depth = GROUPS * TILES * devices
    reverse = np.eye(WIDTH)[::-1].astype(jnp.bfloat16)
    return pl.pallas_call(
        functools.partial(synthesis_kernel, float(truncation)),
        out_shape=jax.ShapeDtypeStruct((8, DENSE, WIDTH), bf16),
        in_specs=[pl.BlockSpec(memory_space=pltpu.SMEM)] + [VMEM_SPEC] * 5,
        out_specs=VMEM_SPEC,
        scratch_shapes=[
            pltpu.VMEM((devices * 4 * TILES, WIDTH), f32),
            pltpu.VMEM((4, 2, ROWS, depth), f32),
            pltpu.VMEM((BATCH * COLUMNS, 2 * depth), bf16),
            pltpu.VMEM((BATCH * COLUMNS, 2 * depth), bf16),
            pltpu.VMEM((2 * COLUMNS * BATCH * BATCHES, WIDTH), f32),
            pltpu.VMEM((2 * COLUMNS * BATCH * BATCHES, WIDTH), f32),
            pltpu.VMEM((4, DENSE, WIDTH), f32),
        ],
        compiler_params=pltpu.CompilerParams(vmem_limit_bytes=16 << 20),
    )(points, received, wave_line, select_rows(), reverse, tables)


def place_kernel(in_ref, out_ref, dense, placed):
    for source in range(in_ref.shape[0]):
        dense[source] = in_ref[source].astype(f32)
        rest = dense[source, 200:208]
        rest = jnp.concatenate([rest, pltpu.roll(rest, WIDTH - 16, 1), pltpu.roll(rest, WIDTH - 32, 1)], axis=0)
        for kind in range(2):
            to = slice(10 * source, 10 * source + 10)
            for i in range(10):
                at = 20 * i + 10 * kind
                placed[kind, to, WIDTH * i : WIDTH * i + WIDTH] = dense[source, at : at + 10]
            placed[kind, to, 10 * WIDTH : QUARTER] = rest[10 * kind : 10 * kind + 10, 0:REST]
    out_ref[...] = placed[:, :, 0:QUARTER].astype(bf16)


def place(blocks):
    sources = blocks.shape[0]
    return pl.pallas_call(
        place_kernel,
        out_shape=jax.ShapeDtypeStruct((2, 10 * sources, QUARTER), bf16),
        in_specs=[VMEM_SPEC],
        out_specs=VMEM_SPEC,
        scratch_shapes=[
            pltpu.VMEM((sources, DENSE, WIDTH), f32),
            pltpu.VMEM((2, 10 * sources, 11 * WIDTH), f32),
        ],
        compiler_params=pltpu.CompilerParams(vmem_limit_bytes=8 << 20),
    )(blocks)


def wave_line_of(index, truncation):
    low = jnp.transpose(index[:, 0, 0:10])
    both = jnp.stack([low, truncation - low], axis=1)
    both = both.reshape(TILES, GROUPS, index.shape[0])
    return jnp.transpose(both, (1, 0, 2)).reshape(1, -1)


def on_device(spectral, legendre, wave_pairs, npoints, lat_rows):
    truncation = legendre.shape[1] - 2
    devices = lax.axis_size("wave")
    index = lax.all_to_all(announcement(wave_pairs, lat_rows, devices), "wave", 0, 0, tiled=True)
    sums = legendre_sums(wave_pairs, spectral, legendre)
    ordered = order_latitudes(index, sums)
    received = lax.all_to_all(ordered, "wave", 0, 0, tiled=True)
    tables, points = fourier_tables(lat_rows, npoints, index, truncation)
    wave_line = wave_line_of(index, float(truncation))
    blocks = synthesis(points, received, wave_line, tables, truncation)
    return place(lax.all_to_all(blocks, "field", 0, 0, tiled=True))


def solution(mesh):
    placed = (P("wave", None, None, "field"), P("wave", None, None), P("wave"), P(), P("wave"))
    return jax.shard_map(
        on_device,
        mesh=mesh,
        in_specs=placed,
        out_specs=P(None, None, ("wave", "field")),
        check_vma=False,
    )
```

```python
import functools

import jax
import jax.numpy as jnp
import numpy as np
from jax import lax
from jax.experimental import pallas as pl
from jax.experimental.pallas import tpu as pltpu
from jax.sharding import PartitionSpec as P

ROW_PAIR = 5156
QUARTER = ROW_PAIR // 4
CHUNK = 256
GROUPS = 5
TILES = 4
ROWS = 24
SIN = (6.283184915155849, -41.3415888250942, 81.59992747560547, -76.6142661520567, 41.34181133252104, -12.469328879159221)
COS = (0.9999992080920543, -19.73897953618229, 64.92862553583919, -85.27120644254374, 58.78833787867872, -21.067254412050286)
f32, bf16, i32 = jnp.float32, jnp.bfloat16, jnp.int32
VMEM_SPEC = pl.BlockSpec(memory_space=pltpu.VMEM)


def legendre_kernel(truncation, waves, spec_hbm, leg_hbm, out_ref, spec_ref, leg_ref, coeffs, found, spec_sems, leg_sems):
    rows = truncation + 2
    slots, fields = spec_ref.shape[0], spec_ref.shape[1]
    main = rows - 1

    def copies(slot):
        return (
            pltpu.make_async_copy(spec_hbm.at[slot], spec_ref.at[slot], spec_sems.at[slot]),
            pltpu.make_async_copy(leg_hbm.at[slot], leg_ref.at[slot], leg_sems.at[slot]),
        )

    for slot in range(slots):
        for copy in copies(slot):
            copy.start()
    coeffs[...] = jnp.zeros_like(coeffs)

    def body(slot, carry):
        for copy in copies(slot):
            copy.wait()
        for field in range(fields):
            coeffs[2 * field : 2 * field + 2, 0:rows] = spec_ref[slot, field]
        split = truncation + 1 - waves[slot]
        row = lax.broadcasted_iota(i32, (1, rows), 1)
        low = row < split
        offset = jnp.where(low, row, row - split)
        sign = jnp.where(offset % 2 == 0, 1.0, -1.0).astype(f32)
        low = jnp.where(low, 1.0, 0.0).astype(f32)
        high = 1.0 - low
        values = coeffs[:, 0:rows]
        stacked = jnp.concatenate([values * mask for mask in (low, low * sign, high, high * sign)], axis=0)
        stacked = stacked.astype(bf16)
        sums = jnp.dot(stacked[:, 0:main], leg_ref[slot, 0:main, :], preferred_element_type=f32)
        last = stacked[:, main:rows].astype(f32) * leg_ref[slot, main:rows, :].astype(f32)
        sums = sums + last
        for half in range(2):
            for side in range(2):
                at = (2 * half + side) * ROWS
                found[2 * slot + half, :, 128 * side : 128 * side + 128] = sums[at : at + ROWS, :]
        return carry

    lax.fori_loop(0, slots, body, 0)
    lats = found.shape[2]
    for t in range(TILES):
        part = found[GROUPS * t : GROUPS * (t + 1)].reshape(GROUPS * ROWS, lats)
        part = jnp.concatenate([part, jnp.zeros((128 - GROUPS * ROWS, lats), f32)], axis=0)
        out_ref[:, 128 * t : 128 * t + 128] = jnp.transpose(part).astype(bf16)


def legendre_sums(wave_pairs, spectral, legendre):
    slots, rows, northern = legendre.shape
    fields = spectral.shape[3]
    parts = pltpu.with_memory_space_constraint(jnp.transpose(spectral, (0, 3, 2, 1)), pltpu.HBM)
    legendre = pltpu.with_memory_space_constraint(legendre, pltpu.HBM)
    return pl.pallas_call(
        functools.partial(legendre_kernel, rows - 2),
        out_shape=pltpu.VMEM((2 * northern, 128 * TILES), bf16),
        in_specs=[pl.BlockSpec(memory_space=pltpu.SMEM)] + [pl.BlockSpec(memory_space=pltpu.HBM)] * 2,
        out_specs=VMEM_SPEC,
        scratch_shapes=[
            pltpu.VMEM((slots, fields, 2, rows), f32),
            pltpu.VMEM((slots, rows, northern), bf16),
            pltpu.VMEM((ROWS, 1408), f32),
            pltpu.VMEM((2 * slots, ROWS, 2 * northern), f32),
            pltpu.SemaphoreType.DMA((slots,)),
            pltpu.SemaphoreType.DMA((slots,)),
        ],
        compiler_params=pltpu.CompilerParams(vmem_limit_bytes=16 << 20),
    )(pltpu.with_memory_space_constraint(wave_pairs, pltpu.HBM), parts, legendre)


def announce_kernel(waves, lats, out_ref):
    lane = lax.broadcasted_iota(i32, (1, 128), 1)
    row = jnp.zeros((1, 128), i32)
    for i in range(14):
        row = jnp.where(lane == i, waves[i] if i < 10 else lats[i - 10], row)
    out_ref[...] = jnp.broadcast_to(row.astype(f32).reshape(1, 1, 128), out_ref.shape)


def announcement(wave_pairs, lat_rows, devices):
    return pl.pallas_call(
        announce_kernel,
        out_shape=jax.ShapeDtypeStruct((devices, 1, 128), f32),
        in_specs=[pl.BlockSpec(memory_space=pltpu.SMEM)] * 2,
        out_specs=VMEM_SPEC,
        compiler_params=pltpu.CompilerParams(vmem_limit_bytes=1 << 20),
    )(*(pltpu.with_memory_space_constraint(x, pltpu.HBM) for x in (wave_pairs, lat_rows)))


def order_kernel(index_ref, sums_ref, out_ref, scratch):
    devices, lats = index_ref.shape[0], sums_ref.shape[0]
    index = index_ref[:, 0, :]
    lane = lax.broadcasted_iota(i32, (devices, lats), 1).astype(f32)
    onehot = jnp.concatenate(
        [jnp.where(index[:, 10 + j : 11 + j] == lane, 1.0, 0.0) for j in range(4)], axis=0
    ).astype(bf16)
    for t in range(TILES):
        picked = jnp.dot(onehot, sums_ref[:, 128 * t : 128 * t + 128], preferred_element_type=f32)
        for j in range(4):
            scratch[pl.ds(j * TILES + t, devices, 4 * TILES), :] = picked[devices * j : devices * (j + 1), :]
    out_ref[...] = scratch[...].reshape(out_ref.shape).astype(bf16)


def order_latitudes(index, sums):
    devices = index.shape[0]
    return pl.pallas_call(
        order_kernel,
        out_shape=jax.ShapeDtypeStruct((devices, 4 * TILES, 128), bf16),
        in_specs=[VMEM_SPEC] * 2,
        out_specs=VMEM_SPEC,
        scratch_shapes=[pltpu.VMEM((devices * 4 * TILES, 128), f32)],
        compiler_params=pltpu.CompilerParams(vmem_limit_bytes=8 << 20),
    )(index, sums)


def poly(coefficients, y):
    total = jnp.full_like(y, coefficients[-1])
    for c in coefficients[-2::-1]:
        total = total * y + c
    return total


def sincos(product, n, inverse):
    turns = jnp.floor(product * inverse + 0.5)
    f = (product - turns * n) * inverse
    y = f * f
    return poly(COS, y), poly(SIN, y) * f


BLOCK = 128


def table_kernel(truncation, lat_rows, npoints, index_ref, out_ref, points_ref, waves):
    l = pl.program_id(0)
    devices = index_ref.shape[0]
    depth = GROUPS * TILES * devices

    @pl.when(l == 0)
    def _():
        index = index_ref[:, 0, :]
        for g in range(GROUPS):
            for t in range(TILES):
                ph = GROUPS * t + g
                column = index[:, ph // 2 : ph // 2 + 1]
                if ph % 2:
                    column = truncation - column
                at = devices * (TILES * g + t)
                waves[at : at + devices, :] = jnp.broadcast_to(column, (devices, 128))

    points_ref[l] = npoints[lat_rows[l]]
    odd = (2 * lax.broadcasted_iota(i32, (BLOCK, 128), 1) + 1).astype(f32)
    n = jnp.full((8, 128), 2 * npoints[lat_rows[l]], i32).astype(f32)
    inverse = (1.0 / n)[0:1]
    n = n[0:1]

    def rows_block(r, carry):
        at = pl.multiple_of(r * BLOCK, BLOCK)
        cosine, sine = sincos(waves[pl.ds(at, BLOCK), :] * odd, n, inverse)
        out_ref[0, pl.ds(at, BLOCK), :] = cosine.astype(bf16)
        out_ref[0, pl.ds(depth + at, BLOCK), :] = sine.astype(bf16)
        return carry

    lax.fori_loop(0, depth // BLOCK, rows_block, 0)


def fourier_tables(lat_rows, npoints, index, truncation):
    devices = index.shape[0]
    depth = GROUPS * TILES * devices
    return pl.pallas_call(
        functools.partial(table_kernel, float(truncation)),
        out_shape=(pltpu.VMEM((4, 2 * depth, CHUNK // 2), bf16), jax.ShapeDtypeStruct((4,), i32)),
        grid_spec=pltpu.PrefetchScalarGridSpec(
            num_scalar_prefetch=2,
            grid=(4,),
            in_specs=[VMEM_SPEC],
            out_specs=(
                pl.BlockSpec((1, 2 * depth, CHUNK // 2), lambda l, a, b: (l, 0, 0)),
                pl.BlockSpec(memory_space=pltpu.SMEM),
            ),
            scratch_shapes=[pltpu.VMEM((depth, 128), f32)],
        ),
        compiler_params=pltpu.CompilerParams(vmem_limit_bytes=8 << 20),
    )(lat_rows, npoints, index)


BATCH = 8
BATCHES = 3
WIDTH = 128
COLUMNS = 20
DENSE = 208
REST = QUARTER - 10 * WIDTH


def synthesis_kernel(
    truncation, points, got_ref, wave_ref, select_ref, reverse_ref, table_ref, out_ref, got, parts, left_0, left_1, line_0, line_1, dense
):
    devices = got_ref.shape[0]
    rows = TILES * devices
    depth = GROUPS * rows
    chunks = BATCH * BATCHES
    got[...] = got_ref[...].reshape(devices * 4 * TILES, WIDTH).astype(f32)
    for l in range(4):
        stacked = jnp.concatenate(
            [got[pl.ds(l * TILES + t, devices, 4 * TILES), :] for t in range(TILES)], axis=0
        ).astype(bf16)
        both = lax.dot_general(select_ref[...], stacked, (((1,), (1,)), ((), ())), preferred_element_type=f32)
        for g in range(GROUPS):
            at = slice(g * rows, (g + 1) * rows)
            row = lax.broadcasted_iota(i32, (ROWS, rows), 0)
            scale = jnp.where(row < 10, 1.0, jnp.broadcast_to(wave_ref[:, at] / truncation, (ROWS, rows)))
            for c in range(2):
                part = both[ROWS * (2 * g + c) : ROWS * (2 * g + c + 1)] * scale
                parts[l, c, :, at] = part.astype(bf16).astype(f32)

    chunk = lax.broadcasted_iota(i32, (BATCH, depth), 0)
    place_in = lax.broadcasted_iota(i32, (BATCH, WIDTH), 0) * CHUNK + lax.broadcasted_iota(i32, (BATCH, WIDTH), 1)
    place_back = lax.broadcasted_iota(i32, (BATCH, WIDTH), 0) * CHUNK - lax.broadcasted_iota(i32, (BATCH, WIDTH), 1)

    lefts, lines = (left_0, left_1), (line_0, line_1)

    def rotate(left, l, first, origin):
        n = jnp.full((8, WIDTH), 2 * points[l], i32).astype(f32)
        inverse = (1.0 / n)[0:1, 0:1]
        n = n[0:1, 0:1]
        center = (2 * CHUNK * (first + chunk) - 2 * origin + CHUNK - 1).astype(f32)
        k = wave_ref[...]
        weight = jnp.where(4.0 * k < n, jnp.where(k == 0.0, 1.0, 2.0), 0.0)
        all_cosine, all_sine = sincos(center * k, n, inverse)
        all_cosine, all_sine = all_cosine * weight, all_sine * weight
        for g in range(GROUPS):
            at = slice(g * rows, (g + 1) * rows)
            at_imag = slice(depth + g * rows, depth + (g + 1) * rows)
            cosine, sine = all_cosine[:, at], all_sine[:, at]
            for f in range(0, COLUMNS, 2):
                turned_real, turned_imag = [], []
                for i in (f, f + 1):
                    real, imag = parts[l, 0, i : i + 1, at], parts[l, 1, i : i + 1, at]
                    turned_real.append(real * cosine - imag * sine)
                    turned_imag.append(imag * cosine + real * sine)
                to = slice(f * BATCH, (f + 2) * BATCH)
                left[to, at] = jnp.concatenate(turned_real, axis=0).astype(bf16)
                left[to, at_imag] = jnp.concatenate(turned_imag, axis=0).astype(bf16)

    def multiply(left, line, l, first, origin):
        even = jnp.dot(left[:, 0:depth], table_ref[l, 0:depth], preferred_element_type=f32)
        odd = jnp.dot(left[:, depth : 2 * depth], table_ref[l, depth : 2 * depth], preferred_element_type=f32)
        before, after = even + odd, even - odd
        limit = origin - CHUNK * first
        keep_back = place_back + (WIDTH - 1) >= limit
        keep_in = place_in + WIDTH >= limit
        for f in range(COLUMNS):
            at = slice(f * BATCH, (f + 1) * BATCH)
            to = pl.ds(pl.multiple_of(f * chunks + first, 8), BATCH)
            line[to] = jnp.where(keep_back, before[at], line[to])
            to = pl.ds(pl.multiple_of((COLUMNS + f) * chunks + first, 8), BATCH)
            line[to] = jnp.where(keep_in, after[at], line[to])

    def body(step, carry):
        at = []
        for pair in range(2):
            n_a = points[2 * pair]
            batches_a = lax.shift_right_arithmetic(n_a - 1, 11) + 1
            start_b = lax.shift_right_arithmetic(n_a, 11)
            second = step >= batches_a
            index = jnp.where(second, jnp.minimum(step - batches_a + start_b, BATCHES - 1), step)
            at.append((2 * pair + jnp.where(second, 1, 0), BATCH * index, jnp.where(second, n_a, 0)))
        for pair in range(2):
            rotate(lefts[pair], *at[pair])
        for pair in range(2):
            multiply(lefts[pair], lines[pair], *at[pair])
        return carry

    lax.fori_loop(0, BATCHES + 1, body, 0, unroll=True)
    lane = lax.broadcasted_iota(i32, (COLUMNS, WIDTH), 1)
    for pair in range(2):
        line = lines[pair]
        back = slice(0, COLUMNS * chunks)
        line[back] = jnp.dot(line[back].astype(bf16), reverse_ref[...], preferred_element_type=f32)

        def tile_of(tile, line=line):
            return line[pl.ds((tile % 2) * COLUMNS * chunks + tile // 2, COLUMNS, chunks), :]

        for q in range(4):
            shift = (QUARTER * q) % WIDTH
            first = QUARTER * q // WIDTH
            ahead = tile_of(first)
            if shift:
                ahead = pltpu.roll(ahead, WIDTH - shift, 1)
            for i in range(QUARTER // WIDTH + 1):
                v = ahead
                if shift or i < QUARTER // WIDTH:
                    ahead = tile_of(first + i + 1)
                if shift:
                    ahead = pltpu.roll(ahead, WIDTH - shift, 1)
                    v = jnp.where(lane < WIDTH - shift, v, ahead)
                if i < 10:
                    dense[q, COLUMNS * i : COLUMNS * i + COLUMNS] = v
                else:
                    dense[q, 200:208] = v[0:8]
                    dense[q, 200:208, 16:32] = v[8:16, 0:16]
                    dense[q, 200:204, 32:48] = v[16:20, 0:16]
            out_ref[4 * pair + q] = dense[q].astype(bf16)


def select_rows():
    table = np.zeros((GROUPS, 2 * ROWS, 128), np.float32)
    for g in range(GROUPS):
        for f in range(10):
            real, imag = g * ROWS + 2 * f, g * ROWS + 2 * f + 1
            table[g, f, real] = 1.0
            table[g, 10 + f, imag] = -1.0
            table[g, ROWS + f, imag] = 1.0
            table[g, ROWS + 10 + f, real] = 1.0
    return table.reshape(GROUPS * 2 * ROWS, 128).astype(jnp.bfloat16)


def synthesis(points, received, wave_line, tables, truncation):
    devices = received.shape[0]
    depth = GROUPS * TILES * devices
    reverse = np.eye(WIDTH)[::-1].astype(jnp.bfloat16)
    return pl.pallas_call(
        functools.partial(synthesis_kernel, float(truncation)),
        out_shape=jax.ShapeDtypeStruct((8, DENSE, WIDTH), bf16),
        in_specs=[pl.BlockSpec(memory_space=pltpu.SMEM)] + [VMEM_SPEC] * 5,
        out_specs=VMEM_SPEC,
        scratch_shapes=[
            pltpu.VMEM((devices * 4 * TILES, WIDTH), f32),
            pltpu.VMEM((4, 2, ROWS, depth), f32),
            pltpu.VMEM((BATCH * COLUMNS, 2 * depth), bf16),
            pltpu.VMEM((BATCH * COLUMNS, 2 * depth), bf16),
            pltpu.VMEM((2 * COLUMNS * BATCH * BATCHES, WIDTH), f32),
            pltpu.VMEM((2 * COLUMNS * BATCH * BATCHES, WIDTH), f32),
            pltpu.VMEM((4, DENSE, WIDTH), f32),
        ],
        compiler_params=pltpu.CompilerParams(vmem_limit_bytes=16 << 20),
    )(points, received, wave_line, select_rows(), reverse, tables)


def place_kernel(in_ref, out_ref, dense, placed):
    for source in range(in_ref.shape[0]):
        dense[source] = in_ref[source].astype(f32)
        rest = dense[source, 200:208]
        rest = jnp.concatenate([rest, pltpu.roll(rest, WIDTH - 16, 1), pltpu.roll(rest, WIDTH - 32, 1)], axis=0)
        for kind in range(2):
            to = slice(10 * source, 10 * source + 10)
            for i in range(10):
                at = 20 * i + 10 * kind
                placed[kind, to, WIDTH * i : WIDTH * i + WIDTH] = dense[source, at : at + 10]
            placed[kind, to, 10 * WIDTH : QUARTER] = rest[10 * kind : 10 * kind + 10, 0:REST]
    out_ref[...] = placed[:, :, 0:QUARTER].astype(bf16)


def place(blocks):
    sources = blocks.shape[0]
    return pl.pallas_call(
        place_kernel,
        out_shape=jax.ShapeDtypeStruct((2, 10 * sources, QUARTER), bf16),
        in_specs=[VMEM_SPEC],
        out_specs=VMEM_SPEC,
        scratch_shapes=[
            pltpu.VMEM((sources, DENSE, WIDTH), f32),
            pltpu.VMEM((2, 10 * sources, 11 * WIDTH), f32),
        ],
        compiler_params=pltpu.CompilerParams(vmem_limit_bytes=8 << 20),
    )(blocks)


def wave_line_of(index, truncation):
    low = jnp.transpose(index[:, 0, 0:10])
    both = jnp.stack([low, truncation - low], axis=1)
    both = both.reshape(TILES, GROUPS, index.shape[0])
    return jnp.transpose(both, (1, 0, 2)).reshape(1, -1)


def on_device(spectral, legendre, wave_pairs, npoints, lat_rows):
    truncation = legendre.shape[1] - 2
    devices = lax.axis_size("wave")
    index = lax.all_to_all(announcement(wave_pairs, lat_rows, devices), "wave", 0, 0, tiled=True)
    sums = legendre_sums(wave_pairs, spectral, legendre)
    ordered = order_latitudes(index, sums)
    received = lax.all_to_all(ordered, "wave", 0, 0, tiled=True)
    tables, points = fourier_tables(lat_rows, npoints, index, truncation)
    wave_line = wave_line_of(index, float(truncation))
    blocks = synthesis(points, received, wave_line, tables, truncation)
    return place(lax.all_to_all(blocks, "field", 0, 0, tiled=True))


def solution(mesh):
    placed = (P("wave", None, None, "field"), P("wave", None, None), P("wave"), P(), P("wave"))
    return jax.shard_map(
        on_device,
        mesh=mesh,
        in_specs=placed,
        out_specs=P(None, None, ("wave", "field")),
        check_vma=False,
    )
```
